512 devices in a mesh: seg: 128 (over x, z, core), lag: 4 (over y).
Axes of the slice: x: 4, y: 4, z: 16, core: 2. Of those that a mesh axis runs over, the one named last changes fastest.
Arguments:
- actuator_input: bfloat16 [393216, 256], P('seg'), may hold values from -24 to 24
- sensor_output: bfloat16 [393216, 2048], P('seg', 'lag'), may hold values from -6 to 6
- run_lengths: int32 [64], replicated, may hold values from 1 to 12288, 393216 in all
- lag_offsets: int32 [2], replicated, may hold values from 0 to 1022, as said below
Outputs:
- markov: float32 [256, 4, 2048], P('seg', 'lag')
The draws below stay inside these ranges and needn't reach their ends.
Inputs may be any that keep to these rules, and one draw needn't show every extreme that they name: `run_lengths`: the 64 lengths add up to 393216; at least one equals 12288. `lag_offsets`: at least one block starts at 1022.
All inputs are finite; a program needn't handle non-finite values.
Results may differ from the reference program's by a relative error of at most 0.0003.
Values may be sent and summed in bfloat16 or wider, within the bound.
A program may use at most 64 MiB of HBM per device.

```python
import math
import jax
import jax.numpy as jnp
import numpy as np
from jax import lax

M = 256
P_SIZE = 2048
TD = 3072
LMAX = 1024
LBW = 2
NBLK = 2
NS = 393216
NSEG = 64
SEG_MOST = 12288


def draw_lag_offsets(key, part):
    first_key, second_key = jax.random.split(jax.random.fold_in(key, 11))
    values = jax.random.randint(first_key, (NBLK,), 0, LMAX - LBW, dtype=jnp.int32)
    place = jax.random.randint(second_key, (), 0, NBLK, dtype=jnp.int32)
    return jnp.where(jnp.arange(NBLK, dtype=jnp.int32) == place, LMAX - LBW, values).astype(jnp.int32)


def with_spikes(array, own_key, source, target, shards_of, factor):
    def block_of(position):
        return (jnp.arange(array.shape[position]) // (array.shape[position] // shards_of)).reshape((-1,) + (1,) * (array.ndim - 1 - position))

    one_side = jax.random.permutation(own_key, shards_of)[block_of(target)]
    other_side = (block_of(target) + shards_of // 2) % shards_of
    return jnp.where((block_of(source) == one_side) | (block_of(source) == other_side), factor * array, array)


def level_of(own_key, dims, cuts, low, largest):
    gain, own = 1.0, jax.random.fold_in(own_key, 6)
    for axis_at, parts in cuts:
        draws = jnp.exp(jax.random.uniform(jax.random.fold_in(own, axis_at), (parts,), jnp.float32, low / len(cuts), largest / len(cuts)))
        gain = gain * jnp.repeat(draws, dims[axis_at] // parts).reshape([-1 if axis == axis_at else 1 for axis in range(len(dims))])
    return gain


def length_profile(number_of, total, reach, lean):
    loads = [(1 << 20) // math.isqrt(standing ** lean) + 1 for standing in range(2, number_of + 1)]
    spare, holding = total - reach - (number_of - 1), [1] * (number_of - 1)
    while spare > 0:
        movable = [i for i in range(number_of - 1) if holding[i] < reach]
        whole, budget = sum([loads[i] for i in movable]), spare
        for i in movable:
            more = min(reach - holding[i], max(1, budget * loads[i] // whole), spare)
            holding[i] = holding[i] + more
            spare = spare - more
    return np.array([reach] + holding)


def uneven_parts(stream_key, number_of, total, reach, lean):
    if number_of == 2:
        one = jax.random.randint(stream_key, (), max(1, total - reach), min(reach, total - 1) + 1)
        return jnp.stack([one, total - one])
    tallies = jnp.asarray(length_profile(number_of, total, reach, lean), jnp.int32)
    couples = (number_of - 1) // 2
    giver, taker = tallies[1:1 + 2 * couples:2], tallies[2:2 + 2 * couples:2]
    margin = jnp.minimum(giver - 1, reach - taker)
    passed = jax.random.randint(jax.random.fold_in(stream_key, 1), (couples,), 0, 1 << 20) % (margin + 1)
    tallies = tallies.at[1:1 + 2 * couples:2].set(giver - passed).at[2:2 + 2 * couples:2].set(taker + passed)
    return tallies[jax.random.permutation(jax.random.fold_in(stream_key, 2), number_of)]


def normal_values(stream_key, dims, scale, reach, cuts=(), kind=jnp.bfloat16):
    values = jax.random.normal(stream_key, dims, jnp.float32) * scale
    if len(cuts) > 0:
        values = level_of(stream_key, dims, cuts, -0.22, 0.18) * values
    return jnp.clip(values, min=-reach, max=reach).astype(kind)


def noise_with(own_key, dims, scale, bound, cuts, heavy, held_as=jnp.bfloat16):
    array = scale * jax.random.normal(own_key, dims, jnp.float32)
    if cuts:
        array = array * level_of(own_key, dims, cuts, -0.22, 0.18)
    return jnp.clip(with_spikes(array, jax.random.fold_in(own_key, 3), *heavy), -bound, bound).astype(held_as)


def setup_inputs(seed: int = 0) -> dict:
    splits = jax.random.split(jax.random.key(seed), 5)
    return {
        "actuator_input": noise_with(splits[0], (NS, M), 1.0, 24.0, ((0, 128),), (0, 1, 128, 5.5)),
        "sensor_output": normal_values(splits[1], (NS, P_SIZE), 1.0, 6.0, ((0, 128), (1, 4))),
        "run_lengths": uneven_parts(splits[2], NSEG, NS, SEG_MOST, 2).astype(jnp.int32),
        "lag_offsets": draw_lag_offsets(jax.random.fold_in(splits[4], 71), 0),
    }


def segment_ids(run_lengths, start_row, row_count):
    run_ends = jnp.cumsum(run_lengths).astype(jnp.int32)
    places = (start_row + jnp.arange(row_count, dtype=jnp.int32)).astype(jnp.int32)
    return lax.optimization_barrier(jnp.sum((run_ends[None, :] <= places[:, None]).astype(jnp.int32), axis=1)).astype(jnp.int32)

def lag_table(lag_offsets):
    offsets_in = jnp.arange(LBW, dtype=jnp.int32)
    return (lag_offsets[:, None] + offsets_in[None, :]).reshape(-1).astype(jnp.int32)

def reference(actuator_input, sensor_output, run_lengths, lag_offsets):
    sample_count = actuator_input.shape[0]
    blocks = sample_count // TD
    idents = segment_ids(run_lengths, 0, sample_count + LMAX)
    shifts = lag_table(lag_offsets)
    actuator_blocks = actuator_input.reshape(blocks, TD, M)
    sensor_blocks = sensor_output.reshape(blocks, TD, P_SIZE)
    next_heads = jnp.concatenate([sensor_blocks[1:, :LMAX], jnp.zeros((1, LMAX, P_SIZE), sensor_output.dtype)], axis=0)

    def add_block(running, inputs):
        actuators, sensors, heads, blk_num = inputs
        joined = jnp.concatenate([sensors, heads], axis=0)
        window_ids = lax.dynamic_slice_in_dim(idents, (blk_num * TD).astype(jnp.int32), TD + LMAX, 0)
        own_ids = window_ids[:TD]

        def lag_product(lag_value):
            shifted = lax.dynamic_slice_in_dim(joined, lag_value, TD, 0)
            shifted_ids = lax.dynamic_slice_in_dim(window_ids, lag_value, TD, 0)
            masked = jnp.where((own_ids == shifted_ids)[:, None], actuators, jnp.zeros_like(actuators))
            return jnp.dot(masked.T, shifted, preferred_element_type=jnp.float32)
        products = lax.map(lag_product, shifts)
        return (running + products, None)
    initial = jnp.zeros((NBLK * LBW, M, P_SIZE), jnp.float32)
    summed, unused = lax.scan(add_block, initial, (actuator_blocks, sensor_blocks, next_heads, jnp.arange(blocks, dtype=jnp.int32)))
    return jnp.transpose(summed, (1, 0, 2)) * (1.0 / math.sqrt(sample_count))
```

```python
import math

import jax
import jax.numpy as jnp
import numpy as np
from jax import lax
from jax.experimental import pallas as pl
from jax.experimental.pallas import tpu as pltpu
from jax.sharding import PartitionSpec as P

LMAX = 1024
LBW = 2
NBLK = 2
NX, NZ, NY, NC = 4, 16, 4, 2
ZL, ZH = 4, 4
F32 = jnp.float32


def device_at(x, z, c, y):
    return (lax.rem(x, NX) * (NZ * NC) + lax.rem(z, NZ) * NC + c, y)


def sums_kernel(part, out, acc, pair, a1, b1, b1h, sa, sb, a2, a2h, b2, stage, fin,
                pair_s, pair_r, a1_s, a1_r, b1_s, b1_r, a2_s, a2_r, b2_s, b2_r, fin_s, fin_r):
    seg, y = lax.axis_index("seg"), lax.axis_index("lag")
    x, z, c = seg // (NZ * NC), lax.rem(seg // NC, NZ), lax.rem(seg, NC)
    zl, zh = lax.rem(z, ZL), z // ZL
    near = [(-1, 0), (1, 1), (2, 2), (-2, 3)]

    def remote(src, dst, send, recv, device):
        return pltpu.make_async_remote_copy(
            src_ref=src, dst_ref=dst, send_sem=send, recv_sem=recv,
            device_id=device, device_id_type=pl.DeviceIdType.MESH)

    barrier = pltpu.get_barrier_semaphore()

    def greet(device):
        pl.semaphore_signal(barrier, inc=1, device_id=device, device_id_type=pl.DeviceIdType.MESH)

    at_home = c == y // 2
    with jax.named_scope("greeting"):
        greet(device_at(x, z, 1 - c, y))
        for dx in range(1, NX):
            greet(device_at(x + dx, z, c, y))
        for step, _ in near:
            greet(device_at(x, z + step + NZ, c, y))
        for q in range(ZH):
            for yy in range(NY):
                source = device_at(x, z + ZL * q, y // 2, lax.rem(y + yy, NY))
                if q == 0 and yy == 0:
                    @pl.when(jnp.logical_not(at_home))
                    def _():
                        greet(source)
                else:
                    greet(source)
        pl.semaphore_wait(barrier, 24 - at_home.astype(jnp.int32))

    waits = []
    with jax.named_scope("pair"):
        pairs = []
        for lag in range(2):
            copy = remote(part.at[2 * (1 - c) + lag], pair.at[lag], pair_s.at[lag], pair_r.at[lag],
                          device_at(x, z, 1 - c, y))
            copy.start()
            pairs.append(copy)
        waits += pairs

    def add_pair(lag):
        @pl.loop(0, NX * ZL)
        def _(i):
            xx, zz = i // ZL, lax.rem(i, ZL)
            acc[lag, xx, zz] = part[2 * c + lag, xx, zz] + pair[lag, xx, zz]

    with jax.named_scope("first"):
        pairs[0].wait_recv()
        add_pair(0)
        x_copies = []
        for dx in (2, 1, 3):
            copy = remote(acc.at[0, lax.rem(x + dx, NX)], a1.at[dx - 1], a1_s.at[dx - 1], a1_r.at[dx - 1],
                          device_at(x + dx, z, c, y))
            copy.start()
            x_copies.append(copy)
        pairs[1].wait_recv()
        add_pair(1)
        z_copies = []
        for step, slot in reversed(near):
            kind = lax.rem(z + step + NZ, ZL)
            if slot < 2:
                src, dst = acc.at[1, :, kind], b1.at[slot]
            else:
                src, dst = acc.at[1, 2 * (slot - 2):2 * (slot - 1), kind], b1h.at[slot - 2]
            copy = remote(src, dst, b1_s.at[slot], b1_r.at[slot], device_at(x, z + step + NZ, c, y))
            copy.start()
            z_copies.append(copy)
        waits += x_copies + z_copies

    with jax.named_scope("second"):
        for copy in x_copies:
            copy.wait_recv()
        for zz in range(ZL):
            sa[zz] = (acc[0, x, zz] + a1[0, zz]) + (a1[1, zz] + a1[2, zz])
        copies_a = []
        for step, slot in reversed(near):
            kind = lax.rem(z + step + NZ, ZL)
            if slot < 2:
                src, dst = sa.at[kind], a2.at[slot]
            else:
                src, dst = sa.at[kind, 8 * (slot - 2):8 * (slot - 1)], a2h.at[slot - 2]
            copy = remote(src, dst, a2_s.at[slot], a2_r.at[slot], device_at(x, z + step + NZ, c, y))
            copy.start()
            copies_a.append(copy)
        for copy in z_copies:
            copy.wait_recv()
        for xx in range(NX):
            sb[xx] = (acc[1, xx, zl] + b1[0, xx]) + (b1[1, xx] + b1h[xx // 2, xx % 2])
        copies_b = []
        for dx in (2, 1, 3):
            copy = remote(sb.at[lax.rem(x + dx, NX)], b2.at[dx - 1], b2_s.at[dx - 1], b2_r.at[dx - 1],
                          device_at(x + dx, z, c, y))
            copy.start()
            copies_b.append(copy)
        waits += copies_a + copies_b

    def send_last(lag):
        for q in (2, 1, 3, 0):
            to_zh = lax.rem(zh + q, ZH)
            for cc in range(NC):
                n = (lag * ZH + q) * NC + cc
                src, dst = stage.at[lag, to_zh, cc], fin.at[zh, y]
                to = device_at(x, z + ZL * q, cc, 2 * c + lag)
                copy = remote(src, dst, fin_s.at[n], fin_r, to)
                if q == 0:
                    mine = (cc == c) & (y == 2 * c + lag)

                    @pl.when(mine)
                    def _():
                        pltpu.make_async_copy(src, dst, fin_r).start()

                    @pl.when(jnp.logical_not(mine))
                    def _():
                        copy.start()
                    last.append((copy, mine))
                else:
                    copy.start()
                    last.append((copy, None))

    with jax.named_scope("third"):
        last = []
        for copy in copies_a:
            copy.wait_recv()
        for half in range(2):
            rows = slice(8 * half, 8 * half + 8)
            total = (sa[zl, rows] + a2[0, rows]) + (a2[1, rows] + a2h[half])
            for k in range(4):
                stage[0, 2 * half + k // 2, k % 2] = total[2 * k:2 * k + 2]
        send_last(0)
        for copy in copies_b:
            copy.wait_recv()
        for half in range(2):
            rows = slice(8 * half, 8 * half + 8)
            total = (sb[x, rows] + b2[0, rows]) + (b2[1, rows] + b2[2, rows])
            for k in range(4):
                stage[1, 2 * half + k // 2, k % 2] = total[2 * k:2 * k + 2]
        send_last(1)

    with jax.named_scope("result"):
        pltpu.make_async_copy(fin, fin, fin_r).wait()
        for yy in range(NY):
            total = (fin[0, yy] + fin[1, yy]) + (fin[2, yy] + fin[3, yy])
            for j in range(2):
                out[j, :, 512 * yy:512 * (yy + 1)] = total[j:j + 1]
        for copy in waits:
            copy.wait_send()
        for copy, mine in last:
            if mine is None:
                copy.wait_send()
            else:
                pl.when(jnp.logical_not(mine))(copy.wait_send)


def summed(part):
    dma = pltpu.SemaphoreType.DMA
    vmem = pltpu.VMEM
    return pl.pallas_call(
        sums_kernel,
        out_shape=jax.ShapeDtypeStruct((2, 1, 2048), F32),
        in_specs=[pl.BlockSpec(memory_space=pltpu.VMEM)],
        out_specs=pl.BlockSpec(memory_space=pltpu.VMEM),
        scratch_shapes=[
            vmem((2, NX, ZL, 16, 512), F32), vmem((2, NX, ZL, 16, 512), F32),
            vmem((3, ZL, 16, 512), F32), vmem((2, NX, 16, 512), F32), vmem((2, 2, 16, 512), F32),
            vmem((ZL, 16, 512), F32), vmem((NX, 16, 512), F32),
            vmem((2, 16, 512), F32), vmem((2, 8, 512), F32), vmem((3, 16, 512), F32),
            vmem((2, ZH, NC, 2, 512), F32), vmem((ZH, NY, 2, 512), F32),
            dma((2,)), dma((2,)), dma((3,)), dma((3,)), dma((4,)), dma((4,)), dma((4,)), dma((4,)),
            dma((3,)), dma((3,)), dma((16,)), dma,
        ],
        compiler_params=pltpu.CompilerParams(collective_id=0, has_side_effects=True,
                                             vmem_limit_bytes=24 << 20),
        name="sums",
    )(part)


def order_of_actuators():
    m = np.arange(256).reshape(NX, ZH, ZL, NC * 2)
    return m.transpose(0, 2, 1, 3).reshape(-1)


def per_device(actuator_input, sensor_output, run_lengths, lag_offsets):
    samples, actuators = actuator_input.shape
    devices_seg = lax.axis_size("seg")
    scaling = 1.0 / math.sqrt(samples * devices_seg)
    start_row = lax.axis_index("seg") * samples
    chosen = jnp.asarray(np.eye(actuators, dtype=np.float32)[:, order_of_actuators()], jnp.bfloat16)
    ordered = jnp.dot(actuator_input, chosen, preferred_element_type=F32).astype(jnp.bfloat16)
    tail = lax.ppermute(ordered[samples - LMAX:], "seg", [(i, i + 1) for i in range(devices_seg - 1)])
    number = run_lengths.shape[0]
    upto = jnp.arange(number)[None, :] <= jnp.arange(number)[:, None]
    run_ends = jnp.sum(jnp.where(upto, run_lengths[None, :], 0), axis=1)
    places = start_row - LMAX + jnp.arange(samples + LMAX, dtype=jnp.int32)
    idents = jnp.sum((run_ends[None, :] <= places[:, None]).astype(jnp.int32), axis=1)
    joined = jnp.concatenate([tail, ordered], axis=0)

    def lag_term(lag_value):
        begin = LMAX - lag_value
        shifted = lax.dynamic_slice_in_dim(joined, begin, samples, 0, allow_negative_indices=False)
        shifted_ids = lax.dynamic_slice_in_dim(idents, begin, samples, 0, allow_negative_indices=False)
        masked = jnp.where((idents[LMAX:] == shifted_ids)[:, None], shifted, jnp.zeros_like(shifted))
        return lax.dot_general(masked, sensor_output, (((0,), (0,)), ((), ())), preferred_element_type=F32)

    shifts = [lag_offsets[blk] + step for blk in range(NBLK) for step in range(LBW)]
    part = jnp.stack([lag_term(lag_value) for lag_value in shifts])
    return summed(part.reshape(4, NX, ZL, 16, 512)) * scaling


def solution(mesh):
    return jax.shard_map(
        per_device,
        mesh=mesh,
        in_specs=(P("seg", None), P("seg", "lag"), P(), P()),
        out_specs=P("seg", "lag", None),
        check_vma=False,
    )
```

```python
import math

import jax
import jax.numpy as jnp
from jax import lax
from jax.experimental import pallas as pl
from jax.experimental.pallas import tpu as pltpu
from jax.sharding import PartitionSpec as P

LMAX = 1024
NX, NZ, NY, NC = 4, 16, 4, 2
ZL, ZH = 4, 4
TD, M, W = 3072, 256, 512
LANES = 128
F32, BF16 = jnp.float32, jnp.bfloat16


def device_at(x, z, c, y):
    return (lax.rem(x, NX) * (NZ * NC) + lax.rem(z, NZ) * NC + c, y)


def kernel(actuators, sensors, lengths, lags, out,
           act, sen, turned, halo, mask, shifts, lhs, part,
           pair, acc, a1, b1, b1h, sa, sb, a2, a2h, b2, stage, fin,
           in_sem, halo_s, halo_r, pair_s, pair_r, a1_s, a1_r, b1_s, b1_r,
           a2_s, a2_r, b2_s, b2_r, fin_s, fin_r):
    seg, y = lax.axis_index("seg"), lax.axis_index("lag")
    x, z, c = seg // (NZ * NC), lax.rem(seg // NC, NZ), lax.rem(seg, NC)
    zl, zh = lax.rem(z, ZL), z // ZL
    near = [(-1, 0), (1, 1), (2, 2), (-2, 3)]
    after = (lax.rem(seg + 1, NX * NZ * NC), y)
    before = (lax.rem(seg + NX * NZ * NC - 1, NX * NZ * NC), y)

    def remote(src, dst, send, recv, device):
        return pltpu.make_async_remote_copy(
            src_ref=src, dst_ref=dst, send_sem=send, recv_sem=recv,
            device_id=device, device_id_type=pl.DeviceIdType.MESH)

    barrier = pltpu.get_barrier_semaphore()

    def greet(device):
        pl.semaphore_signal(barrier, inc=1, device_id=device, device_id_type=pl.DeviceIdType.MESH)

    at_home = c == y // 2
    greet(before)
    loads = []
    for n, (src, dst) in enumerate([
            (actuators.at[TD - LMAX:], act.at[TD - LMAX:]), (actuators.at[:TD - LMAX], act.at[:TD - LMAX]),
            (sensors.at[LMAX:], sen.at[LMAX:]), (sensors.at[:LMAX], sen.at[:LMAX])]):
        copy = pltpu.make_async_copy(src, dst, in_sem.at[n])
        copy.start()
        loads.append(copy)
    greet(device_at(x, z, 1 - c, y))
    for dx in range(1, NX):
        greet(device_at(x + dx, z, c, y))
    for step, _ in near:
        greet(device_at(x, z + step + NZ, c, y))
    for q in range(ZH):
        for yy in range(NY):
            source = device_at(x, z + ZL * q, y // 2, lax.rem(y + yy, NY))
            if q == 0 and yy == 0:
                pl.when(jnp.logical_not(at_home))(lambda source=source: greet(source))
            else:
                greet(source)

    row = lax.broadcasted_iota(jnp.int32, (M, M), 0)
    col = lax.broadcasted_iota(jnp.int32, (M, M), 1)
    wanted = ((row >> 5) & 3) * 64 + (row >> 7) * 32 + ((row >> 2) & 1) * 16 + ((row >> 3) & 3) * 4 + (row & 3)
    order = (col == wanted).astype(F32).astype(BF16)

    def turn(rows):
        flat = lax.dot_general(order, act[rows], (((1,), (1,)), ((), ())), preferred_element_type=F32)
        for i in range(4):
            turned[(LMAX + rows.start) // LANES + i] = flat[:, LANES * i:LANES * i + LANES].astype(BF16)

    loads[0].wait()
    for k in range(4, 6):
        turn(slice(512 * k, 512 * k + 512))
    pl.semaphore_wait(barrier, 25 - at_home.astype(jnp.int32))
    halos = []
    for half in range(2):
        copy = remote(turned.at[TD // LANES:, 128 * half:128 * half + 128], halo.at[half], halo_s.at[half],
                      halo_r.at[half], after)
        copy.start()
        halos.append(copy)

    lane = lax.broadcasted_iota(jnp.int32, (8, TD), 1)
    place = seg * TD + lane

    def step_run(b, carry):
        end, begin = carry
        end = end + lengths[b]
        return end, jnp.where(place >= end, end, begin)

    _, begin = lax.fori_loop(0, 64, step_run, (jnp.int32(0), jnp.zeros((8, TD), jnp.int32)), unroll=8)
    since = place - begin
    for k in range(4):
        mask[k] = jnp.where(since >= lags[k // 2] + k % 2, 1.0, 0.0)
    for b in range(2):
        rest = (LMAX - 1 - lags[b]) & (LANES - 1)
        shifts[b] = (row == (col & (LANES - 1)) + rest + jnp.where(col < LANES, 1, 0)).astype(F32).astype(BF16)
    loads[1].wait()
    for k in range(4):
        turn(slice(512 * k, 512 * k + 512))

    def build(half, first, count):
        rows = slice(128 * half, 128 * half + 128)

        @pl.loop(0, 2)
        def _(b):
            tile = (LMAX - 1 - lags[b]) >> 7
            tiles = [turned[tile + first + j, rows] for j in range(count + 1)]
            windows = [jnp.concatenate(tiles[j:j + 2], axis=1) for j in range(count)]
            moved = jnp.dot(jnp.concatenate(windows, axis=0), shifts[b], preferred_element_type=F32)
            for j in range(count):
                cols = slice(LANES * j, LANES * j + LANES)
                for k in range(2):
                    value = moved[128 * j:128 * j + 128, LANES * k:LANES * k + LANES].reshape(16, 8, LANES)
                    keep = mask[2 * b + k, :, LANES * (first + j):LANES * (first + j + 1)]
                    at = pl.ds(pl.multiple_of(b * 256 + 128 * k, 128), 128)
                    lhs[at, cols] = (value * keep[None]).reshape(128, LANES).astype(BF16)

    def own(half):
        build(half, 8, 16)

        @pl.loop(0, 2)
        def _(n):
            cols = pl.ds(pl.multiple_of(n * 256, 256), 256)
            part[half, :, :, :, :, cols] = jnp.dot(
                lhs[...], sen[LMAX:, cols], preferred_element_type=F32).reshape(4, NX, ZL, 8, 256)

    def cross(half):
        halos[half].wait_recv()
        turned[:LMAX // LANES, 128 * half:128 * half + 128] = halo[half]
        build(half, 0, 8)

        @pl.loop(0, 2)
        def _(n):
            cols = pl.ds(pl.multiple_of(n * 256, 256), 256)
            part[half, :, :, :, :, cols] += jnp.dot(
                lhs[:, :LMAX], sen[:LMAX, cols], preferred_element_type=F32).reshape(4, NX, ZL, 8, 256)

    waits = list(halos)
    pairs, x_first, z_first, x_second, z_second = {}, {}, {}, {}, {}

    def send_pair(half):
        pairs[half] = remote(part.at[half, pl.ds(2 * (1 - c), 2)], pair.at[half], pair_s.at[half],
                             pair_r.at[half], device_at(x, z, 1 - c, y))
        pairs[half].start()
        waits.append(pairs[half])

    def send_first(half):
        pairs[half].wait_recv()
        for lag in range(2):
            @pl.loop(0, NX)
            def _(xx):
                acc[half, lag, xx] = part[half, 2 * c + lag, xx] + pair[half, lag, xx]

            copies = []
            if lag == 0:
                for dx in (2, 1, 3):
                    copies.append(remote(acc.at[half, 0, lax.rem(x + dx, NX)], a1.at[half, dx - 1],
                                         a1_s.at[half, dx - 1], a1_r.at[half, dx - 1], device_at(x + dx, z, c, y)))
                x_first[half] = copies
            else:
                for step, slot in reversed(near):
                    kind = lax.rem(z + step + NZ, ZL)
                    if slot < 2:
                        src, dst = acc.at[half, 1, :, kind], b1.at[half, slot]
                    else:
                        src, dst = acc.at[half, 1, 2 * (slot - 2):2 * (slot - 1), kind], b1h.at[half, slot - 2]
                    copies.append(remote(src, dst, b1_s.at[half, slot], b1_r.at[half, slot],
                                         device_at(x, z + step + NZ, c, y)))
                z_first[half] = copies
            for copy in copies:
                copy.start()
            waits.extend(copies)

    def send_second(half):
        for copy in x_first[half]:
            copy.wait_recv()
        for zz in range(ZL):
            sa[half, zz] = (acc[half, 0, x, zz] + a1[half, 0, zz]) + (a1[half, 1, zz] + a1[half, 2, zz])
        copies = []
        for step, slot in reversed(near):
            kind = lax.rem(z + step + NZ, ZL)
            if slot < 2:
                src, dst = sa.at[half, kind], a2.at[half, slot]
            else:
                src, dst = sa.at[half, kind, :, 256 * (slot - 2):256 * (slot - 1)], a2h.at[half, slot - 2]
            copies.append(remote(src, dst, a2_s.at[half, slot], a2_r.at[half, slot],
                                 device_at(x, z + step + NZ, c, y)))
            copies[-1].start()
        z_second[half] = copies
        waits.extend(copies)
        for copy in z_first[half]:
            copy.wait_recv()
        for xx in range(NX):
            sb[half, xx] = ((acc[half, 1, xx, zl] + b1[half, 0, xx])
                            + (b1[half, 1, xx] + b1h[half, xx // 2, xx % 2]))
        copies = []
        for dx in (2, 1, 3):
            copies.append(remote(sb.at[half, lax.rem(x + dx, NX)], b2.at[half, dx - 1], b2_s.at[half, dx - 1],
                                 b2_r.at[half, dx - 1], device_at(x + dx, z, c, y)))
            copies[-1].start()
        x_second[half] = copies
        waits.extend(copies)

    last = []

    def send_third(half):
        for lag in range(2):
            for copy in (z_second, x_second)[lag][half]:
                copy.wait_recv()
            if lag == 0:
                far = jnp.concatenate([a2h[half, 0], a2h[half, 1]], axis=1)
                total = (sa[half, zl] + a2[half, 0]) + (a2[half, 1] + far)
            else:
                total = (sb[half, x] + b2[half, 0]) + (b2[half, 1] + b2[half, 2])
            for k in range(4):
                stage[half, lag, k // 2, k % 2] = total[2 * k:2 * k + 2]
            for zb in range(2):
                for cc in range(NC):
                    n = ((half * 2 + lag) * 2 + zb) * NC + cc
                    to_zh = 2 * half + zb
                    src, dst = stage.at[half, lag, zb, cc], fin.at[zh, y]
                    copy = remote(src, dst, fin_s.at[n], fin_r, device_at(x, ZL * to_zh + zl, cc, 2 * c + lag))
                    mine = (cc == c) & (y == 2 * c + lag) & (zh == to_zh)

                    @pl.when(mine)
                    def _():
                        pltpu.make_async_copy(src, dst, fin_r).start()

                    @pl.when(jnp.logical_not(mine))
                    def _():
                        copy.start()
                    last.append((copy, mine))

    loads[2].wait()
    own(0)
    loads[3].wait()
    cross(0)
    send_pair(0)
    own(1)
    send_first(0)
    cross(1)
    send_pair(1)
    send_first(1)
    send_second(0)
    send_third(0)
    send_second(1)
    send_third(1)
    pltpu.make_async_copy(fin, fin, fin_r).wait()
    for yy in range(NY):
        total = (fin[0, yy] + fin[1, yy]) + (fin[2, yy] + fin[3, yy])
        for j in range(2):
            out[j, :, W * yy:W * (yy + 1)] = total[j:j + 1]
    for copy in waits:
        copy.wait_send()
    for copy, mine in last:
        pl.when(jnp.logical_not(mine))(copy.wait_send)


def per_device(actuator_input, sensor_output, run_lengths, lag_offsets):
    samples = actuator_input.shape[0]
    scaling = 1.0 / math.sqrt(samples * lax.axis_size("seg"))
    dma, vmem = pltpu.SemaphoreType.DMA, pltpu.VMEM
    anywhere, scalars = pl.BlockSpec(memory_space=pl.ANY), pl.BlockSpec(memory_space=pltpu.SMEM)
    sums = pl.pallas_call(
        kernel,
        out_shape=jax.ShapeDtypeStruct((2, 1, NY * W), F32),
        in_specs=[anywhere, anywhere, scalars, scalars],
        out_specs=pl.BlockSpec(memory_space=pltpu.VMEM),
        scratch_shapes=[
            vmem((TD, M), BF16), vmem((TD, W), BF16), vmem(((LMAX + TD) // LANES, M, LANES), BF16),
            vmem((2, LMAX // LANES, 128, LANES), BF16), vmem((4, 8, TD), F32),
            vmem((2, 256, 256), BF16), vmem((512, 2048), BF16),
            vmem((2, 4, NX, ZL, 8, W), F32),
            vmem((2, 2, NX, ZL, 8, W), F32), vmem((2, 2, NX, ZL, 8, W), F32),
            vmem((2, 3, ZL, 8, W), F32), vmem((2, 2, NX, 8, W), F32), vmem((2, 2, 2, 8, W), F32),
            vmem((2, ZL, 8, W), F32), vmem((2, NX, 8, W), F32),
            vmem((2, 2, 8, W), F32), vmem((2, 2, 8, 256), F32), vmem((2, 3, 8, W), F32),
            vmem((2, 2, 2, NC, 2, W), F32), vmem((ZH, NY, 2, W), F32),
            dma((4,)), dma((2,)), dma((2,)), dma((2,)), dma((2,)), dma((2, 3)), dma((2, 3)),
            dma((2, 4)), dma((2, 4)), dma((2, 4)), dma((2, 4)), dma((2, 3)), dma((2, 3)), dma((16,)), dma,
        ],
        compiler_params=pltpu.CompilerParams(collective_id=0, has_side_effects=True,
                                             vmem_limit_bytes=40 << 20),
        name="correlate",
    )(actuator_input, sensor_output, run_lengths, lag_offsets)
    return sums * scaling


def solution(mesh):
    return jax.shard_map(
        per_device,
        mesh=mesh,
        in_specs=(P("seg", None), P("seg", "lag"), P(), P()),
        out_specs=P("seg", "lag", None),
        check_vma=False,
    )
```

```python
import math

import jax
import jax.numpy as jnp
from jax import lax
from jax.experimental import pallas as pl
from jax.experimental.pallas import tpu as pltpu
from jax.sharding import PartitionSpec as P

LMAX = 1024
NX, NZ, NY, NC = 4, 16, 4, 2
ZL, ZH = 4, 4
TD, M, W = 3072, 256, 512
LANES = 128
F32, BF16 = jnp.float32, jnp.bfloat16


def device_at(x, z, c, y):
    return (lax.rem(x, NX) * (NZ * NC) + lax.rem(z, NZ) * NC + c, y)


def kernel(actuators, sensors, run_lengths, lag_offsets, out,
           lengths, lags, act, sen, turned, halo, mask, shifts, lhs, part,
           pair, acc, a1, b1, b1h, sa, sb, a2, a2h, b2, stage, fin,
           in_sem, halo_s, halo_r, pair_s, pair_r, a1_s, a1_r, b1_s, b1_r,
           a2_s, a2_r, b2_s, b2_r, fin_s, fin_r):
    seg, y = lax.axis_index("seg"), lax.axis_index("lag")
    x, z, c = seg // (NZ * NC), lax.rem(seg // NC, NZ), lax.rem(seg, NC)
    zl, zh = lax.rem(z, ZL), z // ZL
    near = [(-1, 0), (1, 1), (2, 2), (-2, 3)]
    after = (lax.rem(seg + 1, NX * NZ * NC), y)
    before = (lax.rem(seg + NX * NZ * NC - 1, NX * NZ * NC), y)

    def remote(src, dst, send, recv, device):
        return pltpu.make_async_remote_copy(
            src_ref=src, dst_ref=dst, send_sem=send, recv_sem=recv,
            device_id=device, device_id_type=pl.DeviceIdType.MESH)

    barrier = pltpu.get_barrier_semaphore()

    def greet(device):
        pl.semaphore_signal(barrier, inc=1, device_id=device, device_id_type=pl.DeviceIdType.MESH)

    at_home = c == y // 2
    greet(before)
    loads = []
    for n, (src, dst) in enumerate([
            (actuators.at[TD - LMAX:], act.at[TD - LMAX:]), (actuators.at[:TD - LMAX], act.at[:TD - LMAX]),
            (sensors.at[LMAX:], sen.at[LMAX:]), (sensors.at[:LMAX], sen.at[:LMAX]),
            (run_lengths, lengths), (lag_offsets, lags)]):
        copy = pltpu.make_async_copy(src, dst, in_sem.at[n])
        copy.start()
        loads.append(copy)
    greet(device_at(x, z, 1 - c, y))
    for dx in range(1, NX):
        greet(device_at(x + dx, z, c, y))
    for step, _ in near:
        greet(device_at(x, z + step + NZ, c, y))
    for q in range(ZH):
        for yy in range(NY):
            source = device_at(x, z + ZL * q, y // 2, lax.rem(y + yy, NY))
            if q == 0 and yy == 0:
                pl.when(jnp.logical_not(at_home))(lambda source=source: greet(source))
            else:
                greet(source)

    row = lax.broadcasted_iota(jnp.int32, (M, M), 0)
    col = lax.broadcasted_iota(jnp.int32, (M, M), 1)
    wanted = ((row >> 5) & 3) * 64 + (row >> 7) * 32 + ((row >> 2) & 1) * 16 + ((row >> 3) & 3) * 4 + (row & 3)
    order = (col == wanted).astype(F32).astype(BF16)

    def turn(rows):
        flat = lax.dot_general(order, act[rows], (((1,), (1,)), ((), ())), preferred_element_type=F32)
        for i in range(4):
            turned[(LMAX + rows.start) // LANES + i] = flat[:, LANES * i:LANES * i + LANES].astype(BF16)

    loads[0].wait()
    for k in range(4, 6):
        turn(slice(512 * k, 512 * k + 512))
    pl.semaphore_wait(barrier, 25 - at_home.astype(jnp.int32))
    halos = []
    for half in range(2):
        copy = remote(turned.at[TD // LANES:, 128 * half:128 * half + 128], halo.at[half], halo_s.at[half],
                      halo_r.at[half], after)
        copy.start()
        halos.append(copy)

    loads[4].wait()
    loads[5].wait()
    lane = lax.broadcasted_iota(jnp.int32, (8, TD), 1)
    place = seg * TD + lane

    def step_run(b, carry):
        end, begin = carry
        end = end + lengths[b]
        return end, jnp.where(place >= end, end, begin)

    _, begin = lax.fori_loop(0, 64, step_run, (jnp.int32(0), jnp.zeros((8, TD), jnp.int32)), unroll=8)
    since = place - begin
    for k in range(4):
        mask[k] = jnp.where(since >= lags[k // 2] + k % 2, 1.0, 0.0)
    for b in range(2):
        rest = (LMAX - 1 - lags[b]) & (LANES - 1)
        shifts[b] = (row == (col & (LANES - 1)) + rest + jnp.where(col < LANES, 1, 0)).astype(F32).astype(BF16)
    loads[1].wait()
    for k in range(4):
        turn(slice(512 * k, 512 * k + 512))

    def build(half, first, count):
        rows = slice(128 * half, 128 * half + 128)

        @pl.loop(0, 2)
        def _(b):
            tile = (LMAX - 1 - lags[b]) >> 7
            tiles = [turned[tile + first + j, rows] for j in range(count + 1)]
            windows = [jnp.concatenate(tiles[j:j + 2], axis=1) for j in range(count)]
            moved = jnp.dot(jnp.concatenate(windows, axis=0), shifts[b], preferred_element_type=F32)
            for j in range(count):
                cols = slice(LANES * j, LANES * j + LANES)
                for k in range(2):
                    value = moved[128 * j:128 * j + 128, LANES * k:LANES * k + LANES].reshape(16, 8, LANES)
                    keep = mask[2 * b + k, :, LANES * (first + j):LANES * (first + j + 1)]
                    at = pl.ds(pl.multiple_of(b * 256 + 128 * k, 128), 128)
                    lhs[at, cols] = (value * keep[None]).reshape(128, LANES).astype(BF16)

    def own(half):
        build(half, 8, 16)

        @pl.loop(0, 2)
        def _(n):
            cols = pl.ds(pl.multiple_of(n * 256, 256), 256)
            part[half, :, :, :, :, cols] = jnp.dot(
                lhs[...], sen[LMAX:, cols], preferred_element_type=F32).reshape(4, NX, ZL, 8, 256)

    def cross(half):
        halos[half].wait_recv()
        turned[:LMAX // LANES, 128 * half:128 * half + 128] = halo[half]
        build(half, 0, 8)

        @pl.loop(0, 2)
        def _(n):
            cols = pl.ds(pl.multiple_of(n * 256, 256), 256)
            part[half, :, :, :, :, cols] += jnp.dot(
                lhs[:, :LMAX], sen[:LMAX, cols], preferred_element_type=F32).reshape(4, NX, ZL, 8, 256)

    waits = list(halos)
    pairs, x_first, z_first, x_second, z_second = {}, {}, {}, {}, {}

    def send_pair(half):
        pairs[half] = remote(part.at[half, pl.ds(2 * (1 - c), 2)], pair.at[half], pair_s.at[half],
                             pair_r.at[half], device_at(x, z, 1 - c, y))
        pairs[half].start()
        waits.append(pairs[half])

    def send_first(half):
        pairs[half].wait_recv()
        for lag in range(2):
            @pl.loop(0, NX)
            def _(xx):
                acc[half, lag, xx] = part[half, 2 * c + lag, xx] + pair[half, lag, xx]

            copies = []
            if lag == 0:
                for dx in (2, 1, 3):
                    copies.append(remote(acc.at[half, 0, lax.rem(x + dx, NX)], a1.at[half, dx - 1],
                                         a1_s.at[half, dx - 1], a1_r.at[half, dx - 1], device_at(x + dx, z, c, y)))
                x_first[half] = copies
            else:
                for step, slot in reversed(near):
                    kind = lax.rem(z + step + NZ, ZL)
                    if slot < 2:
                        src, dst = acc.at[half, 1, :, kind], b1.at[half, slot]
                    else:
                        src, dst = acc.at[half, 1, 2 * (slot - 2):2 * (slot - 1), kind], b1h.at[half, slot - 2]
                    copies.append(remote(src, dst, b1_s.at[half, slot], b1_r.at[half, slot],
                                         device_at(x, z + step + NZ, c, y)))
                z_first[half] = copies
            for copy in copies:
                copy.start()
            waits.extend(copies)

    def send_second(half):
        for copy in x_first[half]:
            copy.wait_recv()
        for zz in range(ZL):
            sa[half, zz] = (acc[half, 0, x, zz] + a1[half, 0, zz]) + (a1[half, 1, zz] + a1[half, 2, zz])
        copies = []
        for step, slot in reversed(near):
            kind = lax.rem(z + step + NZ, ZL)
            if slot < 2:
                src, dst = sa.at[half, kind], a2.at[half, slot]
            else:
                src, dst = sa.at[half, kind, :, 256 * (slot - 2):256 * (slot - 1)], a2h.at[half, slot - 2]
            copies.append(remote(src, dst, a2_s.at[half, slot], a2_r.at[half, slot],
                                 device_at(x, z + step + NZ, c, y)))
            copies[-1].start()
        z_second[half] = copies
        waits.extend(copies)
        for copy in z_first[half]:
            copy.wait_recv()
        for xx in range(NX):
            sb[half, xx] = ((acc[half, 1, xx, zl] + b1[half, 0, xx])
                            + (b1[half, 1, xx] + b1h[half, xx // 2, xx % 2]))
        copies = []
        for dx in (2, 1, 3):
            copies.append(remote(sb.at[half, lax.rem(x + dx, NX)], b2.at[half, dx - 1], b2_s.at[half, dx - 1],
                                 b2_r.at[half, dx - 1], device_at(x + dx, z, c, y)))
            copies[-1].start()
        x_second[half] = copies
        waits.extend(copies)

    last = []

    def send_third(half):
        for lag in range(2):
            for copy in (z_second, x_second)[lag][half]:
                copy.wait_recv()
            if lag == 0:
                far = jnp.concatenate([a2h[half, 0], a2h[half, 1]], axis=1)
                total = (sa[half, zl] + a2[half, 0]) + (a2[half, 1] + far)
            else:
                total = (sb[half, x] + b2[half, 0]) + (b2[half, 1] + b2[half, 2])
            for k in range(4):
                stage[half, lag, k // 2, k % 2] = total[2 * k:2 * k + 2]
            for zb in range(2):
                for cc in range(NC):
                    n = ((half * 2 + lag) * 2 + zb) * NC + cc
                    to_zh = 2 * half + zb
                    src, dst = stage.at[half, lag, zb, cc], fin.at[zh, y]
                    copy = remote(src, dst, fin_s.at[n], fin_r, device_at(x, ZL * to_zh + zl, cc, 2 * c + lag))
                    mine = (cc == c) & (y == 2 * c + lag) & (zh == to_zh)

                    @pl.when(mine)
                    def _():
                        pltpu.make_async_copy(src, dst, fin_r).start()

                    @pl.when(jnp.logical_not(mine))
                    def _():
                        copy.start()
                    last.append((copy, mine))

    loads[2].wait()
    own(0)
    loads[3].wait()
    cross(0)
    send_pair(0)
    own(1)
    send_first(0)
    cross(1)
    send_pair(1)
    send_first(1)
    send_second(0)
    send_third(0)
    send_second(1)
    send_third(1)
    pltpu.make_async_copy(fin, fin, fin_r).wait()
    for yy in range(NY):
        total = (fin[0, yy] + fin[1, yy]) + (fin[2, yy] + fin[3, yy])
        for j in range(2):
            out[j, :, W * yy:W * (yy + 1)] = total[j:j + 1]
    for copy in waits:
        copy.wait_send()
    for copy, mine in last:
        pl.when(jnp.logical_not(mine))(copy.wait_send)


def per_device(actuator_input, sensor_output, run_lengths, lag_offsets):
    samples = actuator_input.shape[0]
    scaling = 1.0 / math.sqrt(samples * lax.axis_size("seg"))
    dma, vmem = pltpu.SemaphoreType.DMA, pltpu.VMEM
    in_hbm = pl.BlockSpec(memory_space=pltpu.HBM)
    sums = pl.pallas_call(
        kernel,
        out_shape=jax.ShapeDtypeStruct((2, 1, NY * W), F32),
        in_specs=[in_hbm] * 4,
        out_specs=pl.BlockSpec(memory_space=pltpu.VMEM),
        scratch_shapes=[
            pltpu.SMEM((64,), jnp.int32), pltpu.SMEM((2,), jnp.int32),
            vmem((TD, M), BF16), vmem((TD, W), BF16), vmem(((LMAX + TD) // LANES, M, LANES), BF16),
            vmem((2, LMAX // LANES, 128, LANES), BF16), vmem((4, 8, TD), F32),
            vmem((2, 256, 256), BF16), vmem((512, 2048), BF16),
            vmem((2, 4, NX, ZL, 8, W), F32),
            vmem((2, 2, NX, ZL, 8, W), F32), vmem((2, 2, NX, ZL, 8, W), F32),
            vmem((2, 3, ZL, 8, W), F32), vmem((2, 2, NX, 8, W), F32), vmem((2, 2, 2, 8, W), F32),
            vmem((2, ZL, 8, W), F32), vmem((2, NX, 8, W), F32),
            vmem((2, 2, 8, W), F32), vmem((2, 2, 8, 256), F32), vmem((2, 3, 8, W), F32),
            vmem((2, 2, 2, NC, 2, W), F32), vmem((ZH, NY, 2, W), F32),
            dma((6,)), dma((2,)), dma((2,)), dma((2,)), dma((2,)), dma((2, 3)), dma((2, 3)),
            dma((2, 4)), dma((2, 4)), dma((2, 4)), dma((2, 4)), dma((2, 3)), dma((2, 3)), dma((16,)), dma,
        ],
        compiler_params=pltpu.CompilerParams(collective_id=0, has_side_effects=True,
                                             vmem_limit_bytes=56 << 20),
        name="correlate",
    )(actuator_input, sensor_output, run_lengths, lag_offsets)
    return sums * scaling


def solution(mesh):
    return jax.shard_map(
        per_device,
        mesh=mesh,
        in_specs=(P("seg", None), P("seg", "lag"), P(), P()),
        out_specs=P("seg", "lag", None),
        check_vma=False,
    )
```

```python
import math

import jax
import jax.numpy as jnp
from jax import lax
from jax.experimental import pallas as pl
from jax.experimental.pallas import tpu as pltpu
from jax.sharding import PartitionSpec as P

LMAX = 1024
NX, NZ, NY, NC = 4, 16, 4, 2
ZL, ZH = 4, 4
TD, M, W = 3072, 256, 512
LANES = 128
F32, BF16 = jnp.float32, jnp.bfloat16


def device_at(x, z, c, y):
    return (lax.rem(x, NX) * (NZ * NC) + lax.rem(z, NZ) * NC + c, y)


def kernel(actuators, sensors, run_lengths, lag_offsets, out,
           lengths, lags, act, sen, turned, halo, mask, shifts, lhs, part,
           pair, acc, a1, b1, b1h, sa, sb, a2, a2h, b2, stage, fin,
           in_sem, halo_s, halo_r, pair_s, pair_r, a1_s, a1_r, b1_s, b1_r,
           a2_s, a2_r, b2_s, b2_r, fin_s, fin_r, told):
    seg, y = lax.axis_index("seg"), lax.axis_index("lag")
    x, z, c = seg // (NZ * NC), lax.rem(seg // NC, NZ), lax.rem(seg, NC)
    zl, zh = lax.rem(z, ZL), z // ZL
    near = [(-1, 0), (1, 1), (2, 2), (-2, 3)]
    after = (lax.rem(seg + 1, NX * NZ * NC), y)
    before = (lax.rem(seg + NX * NZ * NC - 1, NX * NZ * NC), y)

    def remote(src, dst, send, recv, device):
        return pltpu.make_async_remote_copy(
            src_ref=src, dst_ref=dst, send_sem=send, recv_sem=recv,
            device_id=device, device_id_type=pl.DeviceIdType.MESH)

    barrier = pltpu.get_barrier_semaphore()

    def greet(device):
        pl.semaphore_signal(barrier, inc=1, device_id=device, device_id_type=pl.DeviceIdType.MESH)

    greet(before)
    loads = []
    for n, (src, dst) in enumerate([
            (actuators.at[TD - LMAX:], act.at[TD - LMAX:]), (actuators.at[:TD - LMAX], act.at[:TD - LMAX]),
            (sensors.at[LMAX:], sen.at[LMAX:]), (sensors.at[:LMAX], sen.at[:LMAX]),
            (run_lengths, lengths), (lag_offsets, lags)]):
        copy = pltpu.make_async_copy(src, dst, in_sem.at[n])
        copy.start()
        loads.append(copy)
    greet(device_at(x, z, 1 - c, y))
    for dx in range(1, NX):
        greet(device_at(x + dx, z, c, y))
    for step, _ in near:
        greet(device_at(x, z + step + NZ, c, y))
    for yy in range(1, NY):
        greet(device_at(x, z, c, lax.rem(y + yy, NY)))

    rounds = [
        [device_at(x, z, 1 - c, y)],
        [device_at(x, z + 2, c, y), device_at(x, z + NZ - 2, c, y)],
        [device_at(x, z + 4, c, y), device_at(x, z + NZ - 4, c, y)],
        [device_at(x, z, c, lax.rem(y + yy, NY)) for yy in range(1, NY)],
    ]

    def tell(n):
        for device in rounds[n]:
            pl.semaphore_signal(told.at[n], inc=1, device_id=device, device_id_type=pl.DeviceIdType.MESH)

    def hear(n):
        pl.semaphore_wait(told.at[n], len(rounds[n]))

    row = lax.broadcasted_iota(jnp.int32, (M, M), 0)
    col = lax.broadcasted_iota(jnp.int32, (M, M), 1)
    wanted = ((row >> 5) & 3) * 64 + (row >> 7) * 32 + ((row >> 2) & 1) * 16 + ((row >> 3) & 3) * 4 + (row & 3)
    order = (col == wanted).astype(F32).astype(BF16)

    def turn(rows):
        flat = lax.dot_general(order, act[rows], (((1,), (1,)), ((), ())), preferred_element_type=F32)
        for i in range(4):
            turned[(LMAX + rows.start) // LANES + i] = flat[:, LANES * i:LANES * i + LANES].astype(BF16)

    loads[0].wait()
    for k in range(4, 6):
        turn(slice(512 * k, 512 * k + 512))
    pl.semaphore_wait(barrier, 12)
    halos = []
    for half in range(2):
        copy = remote(turned.at[TD // LANES:, 128 * half:128 * half + 128], halo.at[half], halo_s.at[half],
                      halo_r.at[half], after)
        copy.start()
        halos.append(copy)
    tell(0)

    loads[4].wait()
    loads[5].wait()
    lane = lax.broadcasted_iota(jnp.int32, (8, TD), 1)
    place = seg * TD + lane

    def step_run(b, carry):
        end, begin = carry
        end = end + lengths[b]
        return end, jnp.where(place >= end, end, begin)

    _, begin = lax.fori_loop(0, 64, step_run, (jnp.int32(0), jnp.zeros((8, TD), jnp.int32)), unroll=8)
    since = place - begin
    for k in range(4):
        mask[k] = jnp.where(since >= lags[k // 2] + k % 2, 1.0, 0.0)
    for b in range(2):
        rest = (LMAX - 1 - lags[b]) & (LANES - 1)
        shifts[b] = (row == (col & (LANES - 1)) + rest + jnp.where(col < LANES, 1, 0)).astype(F32).astype(BF16)
    loads[1].wait()
    for k in range(4):
        turn(slice(512 * k, 512 * k + 512))

    def build(half, first, count):
        rows = slice(128 * half, 128 * half + 128)

        @pl.loop(0, 2)
        def _(b):
            tile = (LMAX - 1 - lags[b]) >> 7
            tiles = [turned[tile + first + j, rows] for j in range(count + 1)]
            windows = [jnp.concatenate(tiles[j:j + 2], axis=1) for j in range(count)]
            moved = jnp.dot(jnp.concatenate(windows, axis=0), shifts[b], preferred_element_type=F32)
            for j in range(count):
                cols = slice(LANES * j, LANES * j + LANES)
                for k in range(2):
                    value = moved[128 * j:128 * j + 128, LANES * k:LANES * k + LANES].reshape(16, 8, LANES)
                    keep = mask[2 * b + k, :, LANES * (first + j):LANES * (first + j + 1)]
                    at = pl.ds(pl.multiple_of(b * 256 + 128 * k, 128), 128)
                    lhs[at, cols] = (value * keep[None]).reshape(128, LANES).astype(BF16)

    def own(half):
        build(half, 8, 16)

        @pl.loop(0, 2)
        def _(n):
            cols = pl.ds(pl.multiple_of(n * 256, 256), 256)
            part[half, :, :, :, :, cols] = jnp.dot(
                lhs[...], sen[LMAX:, cols], preferred_element_type=F32).reshape(4, NX, ZL, 8, 256)

    def cross(half):
        halos[half].wait_recv()
        turned[:LMAX // LANES, 128 * half:128 * half + 128] = halo[half]
        build(half, 0, 8)

        @pl.loop(0, 2)
        def _(n):
            cols = pl.ds(pl.multiple_of(n * 256, 256), 256)
            part[half, :, :, :, :, cols] += jnp.dot(
                lhs[:, :LMAX], sen[:LMAX, cols], preferred_element_type=F32).reshape(4, NX, ZL, 8, 256)

    waits = list(halos)
    pairs, x_first, z_first, x_second, z_second = {}, {}, {}, {}, {}

    def send_pair(half):
        pairs[half] = remote(part.at[half, pl.ds(2 * (1 - c), 2)], pair.at[half], pair_s.at[half],
                             pair_r.at[half], device_at(x, z, 1 - c, y))
        pairs[half].start()
        waits.append(pairs[half])

    def send_first(half):
        pairs[half].wait_recv()
        for lag in range(2):
            @pl.loop(0, NX)
            def _(xx):
                acc[half, lag, xx] = part[half, 2 * c + lag, xx] + pair[half, lag, xx]

            copies = []
            if lag == 0:
                for dx in (2, 1, 3):
                    copies.append(remote(acc.at[half, 0, lax.rem(x + dx, NX)], a1.at[half, dx - 1],
                                         a1_s.at[half, dx - 1], a1_r.at[half, dx - 1], device_at(x + dx, z, c, y)))
                x_first[half] = copies
            else:
                for step, slot in reversed(near):
                    kind = lax.rem(z + step + NZ, ZL)
                    if slot < 2:
                        src, dst = acc.at[half, 1, :, kind], b1.at[half, slot]
                    else:
                        src, dst = acc.at[half, 1, 2 * (slot - 2):2 * (slot - 1), kind], b1h.at[half, slot - 2]
                    copies.append(remote(src, dst, b1_s.at[half, slot], b1_r.at[half, slot],
                                         device_at(x, z + step + NZ, c, y)))
                z_first[half] = copies
            for copy in copies:
                copy.start()
            waits.extend(copies)

    def send_second(half):
        for copy in x_first[half]:
            copy.wait_recv()
        for zz in range(ZL):
            sa[half, zz] = (acc[half, 0, x, zz] + a1[half, 0, zz]) + (a1[half, 1, zz] + a1[half, 2, zz])
        copies = []
        for step, slot in reversed(near):
            kind = lax.rem(z + step + NZ, ZL)
            if slot < 2:
                src, dst = sa.at[half, kind], a2.at[half, slot]
            else:
                src, dst = sa.at[half, kind, :, 256 * (slot - 2):256 * (slot - 1)], a2h.at[half, slot - 2]
            copies.append(remote(src, dst, a2_s.at[half, slot], a2_r.at[half, slot],
                                 device_at(x, z + step + NZ, c, y)))
            copies[-1].start()
        z_second[half] = copies
        waits.extend(copies)
        for copy in z_first[half]:
            copy.wait_recv()
        for xx in range(NX):
            sb[half, xx] = ((acc[half, 1, xx, zl] + b1[half, 0, xx])
                            + (b1[half, 1, xx] + b1h[half, xx // 2, xx % 2]))
        copies = []
        for dx in (2, 1, 3):
            copies.append(remote(sb.at[half, lax.rem(x + dx, NX)], b2.at[half, dx - 1], b2_s.at[half, dx - 1],
                                 b2_r.at[half, dx - 1], device_at(x + dx, z, c, y)))
            copies[-1].start()
        x_second[half] = copies
        waits.extend(copies)

    last = []

    def send_third(half):
        for lag in range(2):
            for copy in (z_second, x_second)[lag][half]:
                copy.wait_recv()
            if lag == 0:
                far = jnp.concatenate([a2h[half, 0], a2h[half, 1]], axis=1)
                total = (sa[half, zl] + a2[half, 0]) + (a2[half, 1] + far)
            else:
                total = (sb[half, x] + b2[half, 0]) + (b2[half, 1] + b2[half, 2])
            for k in range(4):
                stage[half, lag, k // 2, k % 2] = total[2 * k:2 * k + 2]
            for zb in range(2):
                for cc in range(NC):
                    n = ((half * 2 + lag) * 2 + zb) * NC + cc
                    to_zh = 2 * half + zb
                    src, dst = stage.at[half, lag, zb, cc], fin.at[zh, y]
                    copy = remote(src, dst, fin_s.at[n], fin_r, device_at(x, ZL * to_zh + zl, cc, 2 * c + lag))
                    mine = (cc == c) & (y == 2 * c + lag) & (zh == to_zh)

                    @pl.when(mine)
                    def _():
                        pltpu.make_async_copy(src, dst, fin_r).start()

                    @pl.when(jnp.logical_not(mine))
                    def _():
                        copy.start()
                    last.append((copy, mine))

    hear(0)
    tell(1)
    loads[2].wait()
    own(0)
    hear(1)
    tell(2)
    loads[3].wait()
    cross(0)
    send_pair(0)
    own(1)
    send_first(0)
    hear(2)
    tell(3)
    cross(1)
    send_pair(1)
    send_first(1)
    send_second(0)
    hear(3)
    send_third(0)
    send_second(1)
    send_third(1)
    pltpu.make_async_copy(fin, fin, fin_r).wait()
    for yy in range(NY):
        total = (fin[0, yy] + fin[1, yy]) + (fin[2, yy] + fin[3, yy])
        for j in range(2):
            out[j, :, W * yy:W * (yy + 1)] = total[j:j + 1]
    for copy in waits:
        copy.wait_send()
    for copy, mine in last:
        pl.when(jnp.logical_not(mine))(copy.wait_send)


def per_device(actuator_input, sensor_output, run_lengths, lag_offsets):
    samples = actuator_input.shape[0]
    scaling = 1.0 / math.sqrt(samples * lax.axis_size("seg"))
    dma, vmem = pltpu.SemaphoreType.DMA, pltpu.VMEM
    in_hbm = pl.BlockSpec(memory_space=pltpu.HBM)
    sums = pl.pallas_call(
        kernel,
        out_shape=jax.ShapeDtypeStruct((2, 1, NY * W), F32),
        in_specs=[in_hbm] * 4,
        out_specs=pl.BlockSpec(memory_space=pltpu.VMEM),
        scratch_shapes=[
            pltpu.SMEM((64,), jnp.int32), pltpu.SMEM((2,), jnp.int32),
            vmem((TD, M), BF16), vmem((TD, W), BF16), vmem(((LMAX + TD) // LANES, M, LANES), BF16),
            vmem((2, LMAX // LANES, 128, LANES), BF16), vmem((4, 8, TD), F32),
            vmem((2, 256, 256), BF16), vmem((512, 2048), BF16),
            vmem((2, 4, NX, ZL, 8, W), F32),
            vmem((2, 2, NX, ZL, 8, W), F32), vmem((2, 2, NX, ZL, 8, W), F32),
            vmem((2, 3, ZL, 8, W), F32), vmem((2, 2, NX, 8, W), F32), vmem((2, 2, 2, 8, W), F32),
            vmem((2, ZL, 8, W), F32), vmem((2, NX, 8, W), F32),
            vmem((2, 2, 8, W), F32), vmem((2, 2, 8, 256), F32), vmem((2, 3, 8, W), F32),
            vmem((2, 2, 2, NC, 2, W), F32), vmem((ZH, NY, 2, W), F32),
            dma((6,)), dma((2,)), dma((2,)), dma((2,)), dma((2,)), dma((2, 3)), dma((2, 3)),
            dma((2, 4)), dma((2, 4)), dma((2, 4)), dma((2, 4)), dma((2, 3)), dma((2, 3)), dma((16,)), dma,
            pltpu.SemaphoreType.REGULAR((4,)),
        ],
        compiler_params=pltpu.CompilerParams(collective_id=0, has_side_effects=True,
                                             vmem_limit_bytes=56 << 20),
        name="correlate",
    )(actuator_input, sensor_output, run_lengths, lag_offsets)
    return sums * scaling


def solution(mesh):
    return jax.shard_map(
        per_device,
        mesh=mesh,
        in_specs=(P("seg", None), P("seg", "lag"), P(), P()),
        out_specs=P("seg", "lag", None),
        check_vma=False,
    )
```

```python
import math

import jax
import jax.numpy as jnp
from jax import lax
from jax.experimental import pallas as pl
from jax.experimental.pallas import tpu as pltpu
from jax.sharding import PartitionSpec as P

LMAX = 1024
NX, NZ, NY, NC = 4, 16, 4, 2
ZL, ZH = 4, 4
TD, M, W = 3072, 256, 512
LANES = 128
HALO = LMAX // LANES
TILES = TD // LANES
F32, BF16 = jnp.float32, jnp.bfloat16


def device_at(x, z, c, y):
    return (lax.rem(x, NX) * (NZ * NC) + lax.rem(z, NZ) * NC + c, lax.rem(y, NY))


def kernel(actuators, sensors, run_lengths, lag_offsets, out,
           lengths, lags, act, sen, head, turned, far, mask, shifts, lhs, part_out, part, pair, acc,
           a1, b1, b1h, sa, sb, a2, a2h, b2, stage, fin,
           in_sem, halo_s, halo_r, core_s, core_r, a1_s, a1_r, b1_s, b1_r,
           a2_s, a2_r, b2_s, b2_r, fin_s, fin_r, told):
    seg, y = lax.axis_index("seg"), lax.axis_index("lag")
    x, z, c = seg // (NZ * NC), lax.rem(seg // NC, NZ), lax.rem(seg, NC)
    zl, zh = lax.rem(z, ZL), z // ZL
    chips = NX * NZ
    near = [(-1, 0), (1, 1), (2, 2), (-2, 3)]
    sibling = device_at(x, z, 1 - c, y)
    first_core, second_core = c == 0, c == 1

    def remote(src, dst, send, recv, device):
        return pltpu.make_async_remote_copy(
            src_ref=src, dst_ref=dst, send_sem=send, recv_sem=recv,
            device_id=device, device_id_type=pl.DeviceIdType.MESH)

    barrier = pltpu.get_barrier_semaphore()

    def signal(semaphore, device):
        pl.semaphore_signal(semaphore, inc=1, device_id=device, device_id_type=pl.DeviceIdType.MESH)

    signal(barrier, (lax.rem(seg // NC + chips - 1, chips) * NC + 1, y))
    loads = []
    for n, (src, dst) in enumerate([
            (actuators.at[TD - LMAX:], act.at[TD - LMAX:]), (actuators.at[:TD - LMAX], act.at[:TD - LMAX]),
            (run_lengths, lengths), (lag_offsets, lags), (sensors, sen)]):
        copy = pltpu.make_async_copy(src, dst, in_sem.at[n])
        copy.start()
        loads.append(copy)
    one_hop = [device_at(x + 1, z, c, y), device_at(x + NX - 1, z, c, y), device_at(x, z + 1, c, y),
               device_at(x, z + NZ - 1, c, y), device_at(x, z, c, y + 1), device_at(x, z, c, y + NY - 1)]
    for device in [sibling] + one_hop:
        signal(barrier, device)

    rounds = [
        one_hop,
        [sibling],
        [device_at(x, z + 2, c, y), device_at(x, z + NZ - 2, c, y)],
        [device_at(x, z + 4, c, y), device_at(x, z + NZ - 4, c, y)],
        [device_at(x, z, c, y + yy) for yy in range(1, NY)],
    ]

    def tell(n):
        for device in rounds[n]:
            signal(told.at[n], device)

    def hear(n):
        pl.semaphore_wait(told.at[n], len(rounds[n]))

    row = lax.broadcasted_iota(jnp.int32, (M, M), 0)
    col = lax.broadcasted_iota(jnp.int32, (M, M), 1)
    wanted = ((row >> 5) & 3) * 64 + (row >> 7) * 32 + ((row >> 2) & 1) * 16 + ((row >> 3) & 3) * 4 + (row & 3)
    order = (col == wanted).astype(F32).astype(BF16)

    def turn(k):
        flat = lax.dot_general(order, act[512 * k:512 * k + 512], (((1,), (1,)), ((), ())),
                               preferred_element_type=F32)
        for i in range(4):
            for half in range(2):
                turned[HALO + 4 * k + i, half] = (
                    flat[128 * half:128 * half + 128, LANES * i:LANES * i + LANES].astype(BF16))

    loads[0].wait()
    turn(4)
    turn(5)
    pl.semaphore_wait(barrier, 7 + 2 * c)
    to_next = lax.rem(seg // NC + 1, chips) * NC
    halos = [remote(turned.at[TILES:, half], far.at[:HALO], halo_s.at[half], halo_r, (to_next + half, y))
             for half in range(2)]
    to_core = [remote(turned.at[TILES:], turned.at[:HALO], core_s.at[0], core_r.at[0], sibling),
               remote(sensors.at[:LMAX], head, core_s.at[1], core_r.at[1], sibling)]
    own_head = pltpu.make_async_copy(sensors.at[:LMAX], head, in_sem.at[5])

    @pl.when(second_core)
    def _():
        for copy in halos:
            copy.start()

    @pl.when(first_core)
    def _():
        for copy in to_core:
            copy.start()
        own_head.start()

    tell(0)

    lane = lax.broadcasted_iota(jnp.int32, (8, TD + LMAX), 1)
    place = jnp.where(lane < TD, seg * TD + lane, (seg - c) * TD + lane - TD)
    loads[2].wait()
    loads[3].wait()

    def step_run(b, carry):
        end, begin = carry
        end = end + lengths[b]
        return end, jnp.where(place >= end, end, begin)

    _, begin = lax.fori_loop(0, 64, step_run, (jnp.int32(0), jnp.zeros((8, TD + LMAX), jnp.int32)), unroll=8)
    since = place - begin
    for k in range(4):
        mask[k] = jnp.where(since >= lags[k // 2] + k % 2, 1.0, 0.0)
    for b in range(2):
        rest = (LMAX - 1 - lags[b]) & (LANES - 1)
        shifts[b] = (row == (col & (LANES - 1)) + rest + jnp.where(col < LANES, 1, 0)).astype(F32).astype(BF16)
    loads[1].wait()
    for k in range(4):
        turn(k)
    far[HALO:] = jnp.zeros((HALO, 128, LANES), BF16)

    def build(tiles_of, b, mask_at, col_at):
        tile = (LMAX - 1 - lags[b]) >> 7
        tiles = [tiles_of(tile + j) for j in range(HALO + 1)]
        windows = [jnp.concatenate(tiles[j:j + 2], axis=1) for j in range(HALO)]
        moved = jnp.dot(jnp.concatenate(windows, axis=0), shifts[b], preferred_element_type=F32)
        for j in range(HALO):
            for k in range(2):
                value = moved[128 * j:128 * j + 128, LANES * k:LANES * k + LANES].reshape(16, 8, LANES)
                keep = mask[2 * b + k, :, mask_at + LANES * j:mask_at + LANES * (j + 1)]
                lhs[256 * b + 128 * k:256 * b + 128 * (k + 1), col_at + LANES * j:col_at + LANES * (j + 1)] = (
                    (value * keep[None]).reshape(128, LANES).astype(BF16))

    def own(half, into):
        for b in range(2):
            for first in range(0, TILES, HALO):
                build(lambda i, first=first: turned[i + first, half], b, LANES * first, LANES * first)

        @pl.loop(0, 2)
        def _(n):
            cols = pl.ds(pl.multiple_of(n * 256, 256), 256)
            into[:, :, :, :, cols] = jnp.dot(
                lhs[...], sen[:, cols], preferred_element_type=F32).reshape(4, NX, ZL, 8, 256)

    hear(0)
    tell(1)

    @pl.when(first_core)
    def _():
        turned[:HALO] = jnp.zeros((HALO, 2, 128, LANES), BF16)

    @pl.when(second_core)
    def _():
        to_core[0].wait_recv()

    loads[4].wait()
    own(1 - c, part_out)
    pairs = remote(part_out, pair, core_s.at[2], core_r.at[2], sibling)
    pairs.start()
    hear(1)
    tell(2)
    own(c, part)
    hear(2)
    tell(3)
    pairs.wait_recv()

    @pl.loop(0, 4)
    def _(k):
        part[k] = part[k] + pair[k]

    @pl.when(first_core)
    def _():
        own_head.wait()

    @pl.when(second_core)
    def _():
        to_core[1].wait_recv()

    halos[0].wait_recv()

    def cross(b):
        build(lambda i: far[i], b, TD, 0)

        @pl.loop(0, 2)
        def _(n):
            cols = pl.ds(pl.multiple_of(n * 256, 256), 256)
            acc[2 * b:2 * b + 2, :, :, :, cols] = jnp.dot(
                lhs[256 * b:256 * b + 256, :LMAX], head[:, cols],
                preferred_element_type=F32).reshape(2, NX, ZL, 8, 256) + part[2 * b:2 * b + 2, :, :, :, cols]

    cross(0)
    x_first = [remote(acc.at[:2, lax.rem(x + dx, NX)], a1.at[dx - 1], a1_s.at[dx - 1], a1_r.at[dx - 1],
                      device_at(x + dx, z, c, y)) for dx in (2, 1, 3)]
    for copy in x_first:
        copy.start()
    cross(1)
    z_first = []
    for step, slot in reversed(near):
        kind = lax.rem(z + step + NZ, ZL)
        if slot < 2:
            src, dst = acc.at[2:, :, kind], b1.at[slot]
        else:
            src, dst = acc.at[slot, :, kind], b1h.at[slot - 2]
        z_first.append(remote(src, dst, b1_s.at[slot], b1_r.at[slot], device_at(x, z + step + NZ, c, y)))
        z_first[-1].start()
    hear(3)
    tell(4)

    for copy in x_first:
        copy.wait_recv()
    for k in range(2):
        for zz in range(ZL):
            sa[k, zz] = (acc[k, x, zz] + a1[0, k, zz]) + (a1[1, k, zz] + a1[2, k, zz])
    z_second = []
    for step, slot in reversed(near):
        kind = lax.rem(z + step + NZ, ZL)
        if slot < 2:
            src, dst = sa.at[:, kind], a2.at[slot]
        else:
            src, dst = sa.at[slot - 2, kind], a2h.at[slot - 2]
        z_second.append(remote(src, dst, a2_s.at[slot], a2_r.at[slot], device_at(x, z + step + NZ, c, y)))
        z_second[-1].start()
    for copy in z_first:
        copy.wait_recv()
    for k in range(2):
        for xx in range(NX):
            sb[k, xx] = (acc[2 + k, xx, zl] + b1[0, k, xx]) + (b1[1, k, xx] + b1h[k, xx])
    x_second = [remote(sb.at[:, lax.rem(x + dx, NX)], b2.at[dx - 1], b2_s.at[dx - 1], b2_r.at[dx - 1],
                       device_at(x + dx, z, c, y)) for dx in (2, 1, 3)]
    for copy in x_second:
        copy.start()

    last = []

    def send_last(k, zb):
        for cc in range(NC):
            n = (k * 2 + zb) * NC + cc
            src, dst = stage.at[k, zb, cc], fin.at[zh, y]
            copy = remote(src, dst, fin_s.at[n], fin_r, device_at(x, ZL * (2 * c + zb) + zl, cc, k))
            mine = (cc == c) & (y == k) & (zh == 2 * c + zb)

            @pl.when(mine)
            def _():
                pltpu.make_async_copy(src, dst, fin_r).start()

            @pl.when(jnp.logical_not(mine))
            def _():
                copy.start()
            last.append((copy, mine))

    def set_out(k, total):
        for i in range(4):
            stage[k, i // 2, i % 2] = total[2 * i:2 * i + 2]

    hear(4)
    for copy in z_second:
        copy.wait_recv()
    for k in range(2):
        set_out(k, (sa[k, zl] + a2[0, k]) + (a2[1, k] + a2h[k]))
        send_last(k, 0)
    for copy in x_second:
        copy.wait_recv()
    for k in range(2):
        set_out(2 + k, (sb[k, x] + b2[0, k]) + (b2[1, k] + b2[2, k]))
        send_last(2 + k, 0)
    for k in range(4):
        send_last(k, 1)

    pairs.wait_send()
    for copy in x_first + z_first + z_second + x_second:
        copy.wait_send()

    @pl.when(second_core)
    def _():
        for copy in halos:
            copy.wait_send()

    @pl.when(first_core)
    def _():
        for copy in to_core:
            copy.wait_send()

    pltpu.make_async_copy(fin, fin, fin_r).wait()
    for yy in range(NY):
        total = (fin[0, yy] + fin[1, yy]) + (fin[2, yy] + fin[3, yy])
        for j in range(2):
            out[j, :, W * yy:W * (yy + 1)] = total[j:j + 1]
    for copy, mine in last:
        pl.when(jnp.logical_not(mine))(copy.wait_send)


def per_device(actuator_input, sensor_output, run_lengths, lag_offsets):
    samples = actuator_input.shape[0]
    scaling = 1.0 / math.sqrt(samples * lax.axis_size("seg"))
    dma, vmem = pltpu.SemaphoreType.DMA, pltpu.VMEM
    operands = [pltpu.with_memory_space_constraint(operand, pltpu.HBM)
                for operand in (actuator_input, sensor_output, run_lengths, lag_offsets)]
    block = (4, NX, ZL, 8, W)
    sums = pl.pallas_call(
        kernel,
        out_shape=jax.ShapeDtypeStruct((2, 1, NY * W), F32),
        in_specs=[pl.BlockSpec(memory_space=pltpu.HBM)] * 4,
        out_specs=pl.BlockSpec(memory_space=pltpu.VMEM),
        scratch_shapes=[
            pltpu.SMEM((64,), jnp.int32), pltpu.SMEM((2,), jnp.int32),
            vmem((TD, M), BF16), vmem((TD, W), BF16), vmem((LMAX, W), BF16),
            vmem((HALO + TILES, 2, 128, LANES), BF16), vmem((2 * HALO, 128, LANES), BF16),
            vmem((4, 8, TD + LMAX), F32), vmem((2, 256, 256), BF16), vmem((512, TD), BF16),
            vmem(block, F32), vmem(block, F32), vmem(block, F32), vmem(block, F32),
            vmem((3, 2, ZL, 8, W), F32), vmem((2, 2, NX, 8, W), F32), vmem((2, NX, 8, W), F32),
            vmem((2, ZL, 8, W), F32), vmem((2, NX, 8, W), F32),
            vmem((2, 2, 8, W), F32), vmem((2, 8, W), F32), vmem((3, 2, 8, W), F32),
            vmem((4, 2, NC, 2, W), F32), vmem((ZH, NY, 2, W), F32),
            dma((6,)), dma((2,)), dma, dma((3,)), dma((3,)), dma((3,)), dma((3,)), dma((4,)), dma((4,)),
            dma((4,)), dma((4,)), dma((3,)), dma((3,)), dma((16,)), dma,
            pltpu.SemaphoreType.REGULAR((5,)),
        ],
        compiler_params=pltpu.CompilerParams(collective_id=0, has_side_effects=True,
                                             vmem_limit_bytes=40 << 20),
        name="correlate",
    )(*operands)
    return sums * scaling


def solution(mesh):
    return jax.shard_map(
        per_device,
        mesh=mesh,
        in_specs=(P("seg", None), P("seg", "lag"), P(), P()),
        out_specs=P("seg", "lag", None),
        check_vma=False,
    )
```

```python
import math

import jax
import jax.numpy as jnp
from jax import lax
from jax.experimental import pallas as pl
from jax.experimental.pallas import tpu as pltpu
from jax.sharding import PartitionSpec as P

LMAX = 1024
NX, NZ, NY, NC = 4, 16, 4, 2
ZL, ZH = 4, 4
TD, M, W = 3072, 256, 512
LANES = 128
HALO = LMAX // LANES
TILES = TD // LANES
ORDER = (0, 1, 3, 2)
F32, BF16 = jnp.float32, jnp.bfloat16


def device_at(x, z, c, y):
    return (lax.rem(x, NX) * (NZ * NC) + lax.rem(z, NZ) * NC + c, lax.rem(y, NY))


def kernel(actuators, sensors, run_lengths, lag_offsets, out,
           lengths, lags, act, sen, turned, halo, mask, shifts, lhs, part, pair, acc,
           a1, b1, b1h, sa, sb, a2, a2h, b2, stage, fin,
           in_sem, halo_s, halo_r, pair_s, pair_r, a1_s, a1_r, b1_s, b1_r,
           a2_s, a2_r, b2_s, b2_r, fin_s, fin_r, told):
    seg, y = lax.axis_index("seg"), lax.axis_index("lag")
    x, z, c = seg // (NZ * NC), lax.rem(seg // NC, NZ), lax.rem(seg, NC)
    zl, zh = lax.rem(z, ZL), z // ZL
    after = (lax.rem(seg + 1, NX * NZ * NC), y)
    before = (lax.rem(seg + NX * NZ * NC - 1, NX * NZ * NC), y)
    near = [(-1, 0), (1, 1), (2, 2), (-2, 3)]
    sibling = device_at(x, z, 1 - c, y)

    def remote(src, dst, send, recv, device):
        return pltpu.make_async_remote_copy(
            src_ref=src, dst_ref=dst, send_sem=send, recv_sem=recv,
            device_id=device, device_id_type=pl.DeviceIdType.MESH)

    barrier = pltpu.get_barrier_semaphore()

    def signal(semaphore, device):
        pl.semaphore_signal(semaphore, inc=1, device_id=device, device_id_type=pl.DeviceIdType.MESH)

    signal(barrier, before)
    loads = []
    for n, (src, dst) in enumerate([
            (actuators.at[TD - LMAX:], act.at[TD - LMAX:]), (actuators.at[:TD - LMAX], act.at[:TD - LMAX]),
            (run_lengths, lengths), (lag_offsets, lags),
            (sensors.at[LMAX:], sen.at[LMAX:]), (sensors.at[:LMAX], sen.at[:LMAX])]):
        copy = pltpu.make_async_copy(src, dst, in_sem.at[n])
        copy.start()
        loads.append(copy)
    one_hop = [device_at(x + 1, z, c, y), device_at(x + NX - 1, z, c, y), device_at(x, z + 1, c, y),
               device_at(x, z + NZ - 1, c, y), device_at(x, z, c, y + 1), device_at(x, z, c, y + NY - 1)]
    for device in [sibling] + one_hop:
        signal(barrier, device)

    rounds = [
        one_hop,
        [sibling],
        [device_at(x, z + 2, c, y), device_at(x, z + NZ - 2, c, y)],
        [device_at(x, z + 4, c, y), device_at(x, z + NZ - 4, c, y)],
        [device_at(x, z, c, y + yy) for yy in range(1, NY)],
    ]

    def tell(n):
        for device in rounds[n]:
            signal(told.at[n], device)

    def hear(n):
        pl.semaphore_wait(told.at[n], len(rounds[n]))

    row = lax.broadcasted_iota(jnp.int32, (M, M), 0)
    col = lax.broadcasted_iota(jnp.int32, (M, M), 1)
    wanted = ((row >> 4) & 3) * 64 + (row >> 6) * 16 + ((row >> 2) & 3) * 4 + (row & 3)
    order = (col == wanted).astype(F32).astype(BF16)

    def turn(k):
        flat = lax.dot_general(order, act[512 * k:512 * k + 512], (((1,), (1,)), ((), ())),
                               preferred_element_type=F32)
        for i in range(4):
            turned[HALO + 4 * k + i] = flat[:, LANES * i:LANES * i + LANES].reshape(ZH, 64, LANES).astype(BF16)

    loads[0].wait()
    turn(4)
    turn(5)
    pl.semaphore_wait(barrier, 8)
    halos = {}
    for q in ORDER:
        halos[q] = remote(turned.at[TILES:, q], halo.at[q], halo_s.at[q], halo_r.at[q], after)
        halos[q].start()
    tell(0)

    lane = lax.broadcasted_iota(jnp.int32, (8, TD), 1)
    lag_of_row = lax.broadcasted_iota(jnp.int32, (8, TD), 0) >> 2
    place = seg * TD + lane
    loads[2].wait()
    loads[3].wait()

    def step_run(b, carry):
        end, begin = carry
        end = end + lengths[b]
        return end, jnp.where(place >= end, end, begin)

    _, begin = lax.fori_loop(0, 64, step_run, (jnp.int32(0), jnp.zeros((8, TD), jnp.int32)), unroll=8)
    since = place - begin
    for b in range(2):
        mask[b] = jnp.where(since >= lags[b] + lag_of_row, 1.0, 0.0)
    for b in range(2):
        rest = (LMAX - 1 - lags[b]) & (LANES - 1)
        shifts[b] = (row == (col & (LANES - 1)) + rest + jnp.where(col < LANES, 1, 0)).astype(F32).astype(BF16)
    loads[1].wait()
    for k in range(4):
        turn(k)
    hear(0)
    tell(1)

    first_rows = lax.broadcasted_iota(jnp.int32, (8, 8, LANES), 1) < 4

    def build(q, first, col_at):
        for b in range(2):
            tile = ((LMAX - 1 - lags[b]) >> 7) + first
            tiles = [turned[tile + j, q] for j in range(HALO + 1)]
            windows = [jnp.concatenate(tiles[j:j + 2], axis=1) for j in range(HALO)]
            moved = jnp.dot(jnp.concatenate(windows, axis=0), shifts[b], preferred_element_type=F32)
            for j in range(HALO):
                keep = mask[b, :, LANES * (first + j):LANES * (first + j + 1)][None]
                one, two = [moved[64 * j:64 * j + 64, LANES * k:LANES * k + LANES].reshape(8, 8, LANES)
                            for k in range(2)]
                even = jnp.where(first_rows, one, pltpu.roll(two, 4, 1)) * keep
                odd = jnp.where(first_rows, pltpu.roll(one, 4, 1), two) * keep
                value = jnp.concatenate([even[:, None], odd[:, None]], axis=1).reshape(128, LANES)
                lhs[128 * b:128 * b + 128, col_at + LANES * j:col_at + LANES * (j + 1)] = value.astype(BF16)

    def own(q):
        for first in (HALO, 2 * HALO):
            build(q, first, LANES * (first - HALO))

        @pl.loop(0, 2)
        def _(n):
            cols = pl.ds(pl.multiple_of(n * 256, 256), 256)
            part[q, :, :, :, :, cols] = jnp.dot(
                lhs[...], sen[LMAX:, cols], preferred_element_type=F32).reshape(2, NX, ZL, 8, 256)

    pairs, x_first, z_first, x_second, z_second, last = {}, {}, {}, {}, {}, []

    def cross(q):
        halos[q].wait_recv()
        turned[:HALO, q] = halo[q]
        build(q, 0, 0)

        @pl.loop(0, 2)
        def _(n):
            cols = pl.ds(pl.multiple_of(n * 256, 256), 256)
            part[q, :, :, :, :, cols] += jnp.dot(
                lhs[:, :LMAX], sen[:LMAX, cols], preferred_element_type=F32).reshape(2, NX, ZL, 8, 256)

        pairs[q] = remote(part.at[q, 1 - c], pair.at[q], pair_s.at[q], pair_r.at[q], sibling)
        pairs[q].start()

    def started(copies):
        for copy in copies:
            copy.start()
        return copies

    def send_first(q):
        pairs[q].wait_recv()
        acc[q, :, :, :, :256] = part[q, c, :, :, :, :256] + pair[q, :, :, :, :256]
        x_first[q] = started([
            remote(acc.at[q, lax.rem(x + dx, NX), :, :, :256], a1.at[q, dx - 1], a1_s.at[q, dx - 1],
                   a1_r.at[q, dx - 1], device_at(x + dx, z, c, y)) for dx in (2, 1, 3)])
        acc[q, :, :, :, 256:] = part[q, c, :, :, :, 256:] + pair[q, :, :, :, 256:]
        copies = []
        for step, slot in reversed(near):
            kind = lax.rem(z + step + NZ, ZL)
            if slot < 2:
                src, dst = acc.at[q, :, kind, :, 256:], b1.at[q, slot]
            else:
                src, dst = acc.at[q, 2 * (slot - 2):2 * (slot - 1), kind, :, 256:], b1h.at[q, slot - 2]
            copies.append(remote(src, dst, b1_s.at[q, slot], b1_r.at[q, slot],
                                 device_at(x, z + step + NZ, c, y)))
        z_first[q] = started(copies)

    def send_second(q):
        for copy in x_first[q]:
            copy.wait_recv()
        for zz in range(ZL):
            sa[q, zz] = (acc[q, x, zz, :, :256] + a1[q, 0, zz]) + (a1[q, 1, zz] + a1[q, 2, zz])
        copies = []
        for step, slot in reversed(near):
            kind = lax.rem(z + step + NZ, ZL)
            if slot < 2:
                src, dst = sa.at[q, kind], a2.at[q, slot]
            else:
                src, dst = sa.at[q, kind, :, 128 * (slot - 2):128 * (slot - 1)], a2h.at[q, slot - 2]
            copies.append(remote(src, dst, a2_s.at[q, slot], a2_r.at[q, slot],
                                 device_at(x, z + step + NZ, c, y)))
        z_second[q] = started(copies)
        for copy in z_first[q]:
            copy.wait_recv()
        for xx in range(NX):
            sb[q, xx] = ((acc[q, xx, zl, :, 256:] + b1[q, 0, xx]) + (b1[q, 1, xx] + b1h[q, xx // 2, xx % 2]))
        x_second[q] = started([
            remote(sb.at[q, lax.rem(x + dx, NX)], b2.at[q, dx - 1], b2_s.at[q, dx - 1], b2_r.at[q, dx - 1],
                   device_at(x + dx, z, c, y)) for dx in (2, 1, 3)])

    def send_third(q):
        for copy in z_second[q]:
            copy.wait_recv()
        left = (sa[q, zl] + a2[q, 0]) + (a2[q, 1] + jnp.concatenate([a2h[q, 0], a2h[q, 1]], axis=1))
        for copy in x_second[q]:
            copy.wait_recv()
        right = (sb[q, x] + b2[q, 0]) + (b2[q, 1] + b2[q, 2])
        total = jnp.concatenate([left, right], axis=1)
        for k in range(2):
            for cc in range(NC):
                stage[q, k, cc] = total[4 * k + 2 * cc:4 * k + 2 * cc + 2]
                src, dst = stage.at[q, k, cc], fin.at[zh, y]
                copy = remote(src, dst, fin_s.at[4 * q + 2 * k + cc], fin_r,
                              device_at(x, ZL * q + zl, cc, 2 * c + k))
                mine = (cc == c) & (y == 2 * c + k) & (zh == q)

                @pl.when(mine)
                def _():
                    pltpu.make_async_copy(src, dst, fin_r).start()

                @pl.when(jnp.logical_not(mine))
                def _():
                    copy.start()
                last.append((copy, mine))

    q0, q1, q2, q3 = ORDER
    loads[4].wait()
    own(q0)
    hear(1)
    tell(2)
    own(q1)
    loads[5].wait()
    cross(q0)
    own(q2)
    send_first(q0)
    cross(q1)
    hear(2)
    tell(3)
    own(q3)
    send_first(q1)
    cross(q2)
    send_first(q2)
    send_second(q0)
    cross(q3)
    send_second(q1)
    hear(3)
    tell(4)
    send_first(q3)
    hear(4)
    send_third(q0)
    send_second(q2)
    send_third(q1)
    send_second(q3)
    send_third(q2)
    send_third(q3)
    for q in ORDER:
        for copy in [halos[q], pairs[q]] + x_first[q] + z_first[q] + x_second[q] + z_second[q]:
            copy.wait_send()
    pltpu.make_async_copy(fin, fin, fin_r).wait()
    for yy in range(NY):
        total = (fin[0, yy] + fin[1, yy]) + (fin[2, yy] + fin[3, yy])
        for j in range(2):
            out[j, :, W * yy:W * (yy + 1)] = total[j:j + 1]
    for copy, mine in last:
        pl.when(jnp.logical_not(mine))(copy.wait_send)


def per_device(actuator_input, sensor_output, run_lengths, lag_offsets):
    samples = actuator_input.shape[0]
    scaling = 1.0 / math.sqrt(samples * lax.axis_size("seg"))
    dma, vmem = pltpu.SemaphoreType.DMA, pltpu.VMEM
    operands = [pltpu.with_memory_space_constraint(operand, pltpu.HBM)
                for operand in (actuator_input, sensor_output, run_lengths, lag_offsets)]
    sums = pl.pallas_call(
        kernel,
        out_shape=jax.ShapeDtypeStruct((2, 1, NY * W), F32),
        in_specs=[pl.BlockSpec(memory_space=pltpu.HBM)] * 4,
        out_specs=pl.BlockSpec(memory_space=pltpu.VMEM),
        scratch_shapes=[
            pltpu.SMEM((64,), jnp.int32), pltpu.SMEM((2,), jnp.int32),
            vmem((TD, M), BF16), vmem((TD, W), BF16), vmem((HALO + TILES, ZH, 64, LANES), BF16),
            vmem((ZH, HALO, 64, LANES), BF16), vmem((2, 8, TD), F32), vmem((2, 256, 256), BF16),
            vmem((256, TD - LMAX), BF16), vmem((ZH, 2, NX, ZL, 8, W), F32),
            vmem((ZH, NX, ZL, 8, W), F32), vmem((ZH, NX, ZL, 8, W), F32),
            vmem((ZH, 3, ZL, 8, 256), F32), vmem((ZH, 2, NX, 8, 256), F32), vmem((ZH, 2, 2, 8, 256), F32),
            vmem((ZH, ZL, 8, 256), F32), vmem((ZH, NX, 8, 256), F32),
            vmem((ZH, 2, 8, 256), F32), vmem((ZH, 2, 8, 128), F32), vmem((ZH, 3, 8, 256), F32),
            vmem((ZH, 2, NC, 2, W), F32), vmem((ZH, NY, 2, W), F32),
            dma((6,)), dma((ZH,)), dma((ZH,)), dma((ZH,)), dma((ZH,)), dma((ZH, 3)), dma((ZH, 3)),
            dma((ZH, 4)), dma((ZH, 4)), dma((ZH, 4)), dma((ZH, 4)), dma((ZH, 3)), dma((ZH, 3)), dma((16,)), dma,
            pltpu.SemaphoreType.REGULAR((5,)),
        ],
        compiler_params=pltpu.CompilerParams(collective_id=0, has_side_effects=True,
                                             vmem_limit_bytes=40 << 20),
        name="correlate",
    )(*operands)
    return sums * scaling


def solution(mesh):
    return jax.shard_map(
        per_device,
        mesh=mesh,
        in_specs=(P("seg", None), P("seg", "lag"), P(), P()),
        out_specs=P("seg", "lag", None),
        check_vma=False,
    )
```

```python
import math

import jax
import jax.numpy as jnp
from jax import lax
from jax.experimental import pallas as pl
from jax.experimental.pallas import tpu as pltpu
from jax.sharding import PartitionSpec as P

LMAX = 1024
NX, NZ, NY, NC = 4, 16, 4, 2
ZL, ZH = 4, 4
TD, M, W = 3072, 256, 512
LANES = 128
HALO = LMAX // LANES
TILES = TD // LANES
ORDER = (0, 1, 3, 2)
F32, BF16 = jnp.float32, jnp.bfloat16


def device_at(x, z, c, y):
    return (lax.rem(x, NX) * (NZ * NC) + lax.rem(z, NZ) * NC + c, lax.rem(y, NY))


def kernel(actuators, sensors, run_lengths, lag_offsets, out,
           lengths, lags, act, sen, turned, halo, mask, shifts, lhs, part, pair, acc,
           a1, b1, b1h, sa, sb, a2, a2h, b2, stage, fin,
           in_sem, halo_s, halo_r, pair_s, pair_r, a1_s, a1_r, b1_s, b1_r,
           a2_s, a2_r, b2_s, b2_r, fin_s, fin_r, told):
    seg, y = lax.axis_index("seg"), lax.axis_index("lag")
    x, z, c = seg // (NZ * NC), lax.rem(seg // NC, NZ), lax.rem(seg, NC)
    zl, zh = lax.rem(z, ZL), z // ZL
    after = (lax.rem(seg + 1, NX * NZ * NC), y)
    before = (lax.rem(seg + NX * NZ * NC - 1, NX * NZ * NC), y)
    near = [(-1, 0), (1, 1), (2, 2), (-2, 3)]
    sibling = device_at(x, z, 1 - c, y)

    def remote(src, dst, send, recv, device):
        return pltpu.make_async_remote_copy(
            src_ref=src, dst_ref=dst, send_sem=send, recv_sem=recv,
            device_id=device, device_id_type=pl.DeviceIdType.MESH)

    barrier = pltpu.get_barrier_semaphore()

    def signal(semaphore, device):
        pl.semaphore_signal(semaphore, inc=1, device_id=device, device_id_type=pl.DeviceIdType.MESH)

    signal(barrier, before)
    loads = []
    for n, (src, dst) in enumerate([
            (actuators.at[TD - LMAX:], act.at[TD - LMAX:]), (actuators.at[:TD - LMAX], act.at[:TD - LMAX]),
            (run_lengths, lengths), (lag_offsets, lags),
            (sensors.at[LMAX:], sen.at[LMAX:]), (sensors.at[:LMAX], sen.at[:LMAX])]):
        copy = pltpu.make_async_copy(src, dst, in_sem.at[n])
        copy.start()
        loads.append(copy)
    one_hop = [device_at(x + 1, z, c, y), device_at(x + NX - 1, z, c, y), device_at(x, z + 1, c, y),
               device_at(x, z + NZ - 1, c, y), device_at(x, z, c, y + 1), device_at(x, z, c, y + NY - 1)]
    for device in [sibling] + one_hop:
        signal(barrier, device)

    rounds = [
        one_hop,
        [device_at(x, z + 2, c, y), device_at(x, z + NZ - 2, c, y), sibling],
        [device_at(x, z + 4, c, y), device_at(x, z + NZ - 4, c, y)],
        [sibling] + [device_at(x, z, cc, y + yy) for yy in range(1, NY) for cc in (c, 1 - c)],
    ]

    def tell(n):
        for device in rounds[n]:
            signal(told.at[n], device)

    def hear(n):
        pl.semaphore_wait(told.at[n], len(rounds[n]))

    row = lax.broadcasted_iota(jnp.int32, (M, M), 0)
    col = lax.broadcasted_iota(jnp.int32, (M, M), 1)
    wanted = ((row >> 4) & 3) * 64 + (row >> 6) * 16 + ((row >> 2) & 3) * 4 + (row & 3)
    order = (col == wanted).astype(F32).astype(BF16)

    def turn(k):
        flat = lax.dot_general(order, act[512 * k:512 * k + 512], (((1,), (1,)), ((), ())),
                               preferred_element_type=F32)
        for i in range(4):
            turned[HALO + 4 * k + i] = flat[:, LANES * i:LANES * i + LANES].reshape(ZH, 64, LANES).astype(BF16)

    loads[0].wait()
    turn(4)
    turn(5)
    pl.semaphore_wait(barrier, 8)
    halos = {}
    for q in ORDER:
        halos[q] = remote(turned.at[TILES:, q], halo.at[q], halo_s.at[q], halo_r.at[q], after)
        halos[q].start()
    tell(0)

    lane = lax.broadcasted_iota(jnp.int32, (8, TD), 1)
    lag_of_row = lax.broadcasted_iota(jnp.int32, (8, TD), 0) >> 2
    place = seg * TD + lane
    loads[2].wait()
    loads[3].wait()

    def step_run(b, carry):
        end, begin = carry
        end = end + lengths[b]
        return end, jnp.where(place >= end, end, begin)

    _, begin = lax.fori_loop(0, 64, step_run, (jnp.int32(0), jnp.zeros((8, TD), jnp.int32)), unroll=8)
    since = place - begin
    for b in range(2):
        mask[b] = jnp.where(since >= lags[b] + lag_of_row, 1.0, 0.0)
    for b in range(2):
        rest = (LMAX - 1 - lags[b]) & (LANES - 1)
        shifts[b] = (row == (col & (LANES - 1)) + rest + jnp.where(col < LANES, 1, 0)).astype(F32).astype(BF16)
    loads[1].wait()
    for k in range(4):
        turn(k)
    hear(0)
    tell(1)

    first_rows = lax.broadcasted_iota(jnp.int32, (8, 8, LANES), 1) < 4

    def build(q, first, col_at):
        for b in range(2):
            tile = ((LMAX - 1 - lags[b]) >> 7) + first
            tiles = [turned[tile + j, q] for j in range(HALO + 1)]
            windows = [jnp.concatenate(tiles[j:j + 2], axis=1) for j in range(HALO)]
            moved = jnp.dot(jnp.concatenate(windows, axis=0), shifts[b], preferred_element_type=F32)
            for j in range(HALO):
                keep = mask[b, :, LANES * (first + j):LANES * (first + j + 1)][None]
                one, two = [moved[64 * j:64 * j + 64, LANES * k:LANES * k + LANES].reshape(8, 8, LANES)
                            for k in range(2)]
                even = jnp.where(first_rows, one, pltpu.roll(two, 4, 1)) * keep
                odd = jnp.where(first_rows, pltpu.roll(one, 4, 1), two) * keep
                value = jnp.concatenate([even[:, None], odd[:, None]], axis=1).reshape(128, LANES)
                lhs[128 * b:128 * b + 128, col_at + LANES * j:col_at + LANES * (j + 1)] = value.astype(BF16)

    def own(q):
        for first in (HALO, 2 * HALO):
            build(q, first, LANES * (first - HALO))

        @pl.loop(0, 2)
        def _(n):
            cols = pl.ds(pl.multiple_of(n * 256, 256), 256)
            part[q, :, :, :, :, cols] = jnp.dot(
                lhs[...], sen[LMAX:, cols], preferred_element_type=F32).reshape(2, NX, ZL, 8, 256)

    pairs, x_first, z_first, x_second, z_second, last = {}, {}, {}, {}, {}, []

    def cross(q):
        halos[q].wait_recv()
        turned[:HALO, q] = halo[q]
        build(q, 0, 0)

        @pl.loop(0, 2)
        def _(n):
            cols = pl.ds(pl.multiple_of(n * 256, 256), 256)
            part[q, :, :, :, :, cols] += jnp.dot(
                lhs[:, :LMAX], sen[:LMAX, cols], preferred_element_type=F32).reshape(2, NX, ZL, 8, 256)

        pairs[q] = remote(part.at[q, 1 - c], pair.at[q], pair_s.at[q], pair_r.at[q], sibling)
        pairs[q].start()

    def started(copies):
        for copy in copies:
            copy.start()
        return copies

    def send_first(q):
        pairs[q].wait_recv()
        acc[q, :, :, :, :256] = part[q, c, :, :, :, :256] + pair[q, :, :, :, :256]
        x_first[q] = started([
            remote(acc.at[q, lax.rem(x + dx, NX), :, :, :256], a1.at[q, dx - 1], a1_s.at[q, dx - 1],
                   a1_r.at[q, dx - 1], device_at(x + dx, z, c, y)) for dx in (2, 1, 3)])
        acc[q, :, :, :, 256:] = part[q, c, :, :, :, 256:] + pair[q, :, :, :, 256:]
        copies = []
        for step, slot in reversed(near):
            kind = lax.rem(z + step + NZ, ZL)
            if slot < 2:
                src, dst = acc.at[q, :, kind, :, 256:], b1.at[q, slot]
            else:
                src, dst = acc.at[q, 2 * (slot - 2):2 * (slot - 1), kind, :, 256:], b1h.at[q, slot - 2]
            copies.append(remote(src, dst, b1_s.at[q, slot], b1_r.at[q, slot],
                                 device_at(x, z + step + NZ, c, y)))
        z_first[q] = started(copies)

    def send_second(q):
        for copy in x_first[q]:
            copy.wait_recv()
        for zz in range(ZL):
            sa[q, zz] = (acc[q, x, zz, :, :256] + a1[q, 0, zz]) + (a1[q, 1, zz] + a1[q, 2, zz])
        copies = []
        for step, slot in reversed(near):
            kind = lax.rem(z + step + NZ, ZL)
            if slot < 2:
                src, dst = sa.at[q, kind], a2.at[q, slot]
            else:
                src, dst = sa.at[q, kind, :, 128 * (slot - 2):128 * (slot - 1)], a2h.at[q, slot - 2]
            copies.append(remote(src, dst, a2_s.at[q, slot], a2_r.at[q, slot],
                                 device_at(x, z + step + NZ, c, y)))
        z_second[q] = started(copies)
        for copy in z_first[q]:
            copy.wait_recv()
        for xx in range(NX):
            sb[q, xx] = ((acc[q, xx, zl, :, 256:] + b1[q, 0, xx]) + (b1[q, 1, xx] + b1h[q, xx // 2, xx % 2]))
        x_second[q] = started([
            remote(sb.at[q, lax.rem(x + dx, NX)], b2.at[q, dx - 1], b2_s.at[q, dx - 1], b2_r.at[q, dx - 1],
                   device_at(x + dx, z, c, y)) for dx in (2, 1, 3)])

    def send_third(q):
        for copy in z_second[q]:
            copy.wait_recv()
        left = (sa[q, zl] + a2[q, 0]) + (a2[q, 1] + jnp.concatenate([a2h[q, 0], a2h[q, 1]], axis=1))
        for copy in x_second[q]:
            copy.wait_recv()
        right = (sb[q, x] + b2[q, 0]) + (b2[q, 1] + b2[q, 2])
        total = jnp.concatenate([left, right], axis=1)
        for k in range(2):
            for cc in range(NC):
                stage[q, k, cc] = total[4 * k + 2 * cc:4 * k + 2 * cc + 2]
                src, dst = stage.at[q, k, cc], fin.at[zh, y]
                copy = remote(src, dst, fin_s.at[4 * q + 2 * k + cc], fin_r,
                              device_at(x, ZL * q + zl, cc, 2 * c + k))
                mine = (cc == c) & (y == 2 * c + k) & (zh == q)

                @pl.when(mine)
                def _():
                    pltpu.make_async_copy(src, dst, fin_r).start()

                @pl.when(jnp.logical_not(mine))
                def _():
                    copy.start()
                last.append((copy, mine))

    q0, q1, q2, q3 = ORDER
    loads[4].wait()
    own(q0)
    loads[5].wait()
    cross(q0)
    hear(1)
    tell(2)
    own(q1)
    send_first(q0)
    cross(q1)
    own(q2)
    send_first(q1)
    cross(q2)
    hear(2)
    tell(3)
    own(q3)
    send_second(q0)
    send_first(q2)
    hear(3)
    send_third(q0)
    cross(q3)
    send_second(q1)
    send_first(q3)
    send_third(q1)
    send_second(q2)
    send_third(q2)
    send_second(q3)
    send_third(q3)
    for q in ORDER:
        for copy in [halos[q], pairs[q]] + x_first[q] + z_first[q] + x_second[q] + z_second[q]:
            copy.wait_send()
    pltpu.make_async_copy(fin, fin, fin_r).wait()
    for yy in range(NY):
        total = (fin[0, yy] + fin[1, yy]) + (fin[2, yy] + fin[3, yy])
        for j in range(2):
            out[j, :, W * yy:W * (yy + 1)] = total[j:j + 1]
    for copy, mine in last:
        pl.when(jnp.logical_not(mine))(copy.wait_send)


def per_device(actuator_input, sensor_output, run_lengths, lag_offsets):
    samples = actuator_input.shape[0]
    scaling = 1.0 / math.sqrt(samples * lax.axis_size("seg"))
    dma, vmem = pltpu.SemaphoreType.DMA, pltpu.VMEM
    operands = [pltpu.with_memory_space_constraint(operand, pltpu.HBM)
                for operand in (actuator_input, sensor_output, run_lengths, lag_offsets)]
    sums = pl.pallas_call(
        kernel,
        out_shape=jax.ShapeDtypeStruct((2, 1, NY * W), F32),
        in_specs=[pl.BlockSpec(memory_space=pltpu.HBM)] * 4,
        out_specs=pl.BlockSpec(memory_space=pltpu.VMEM),
        scratch_shapes=[
            pltpu.SMEM((64,), jnp.int32), pltpu.SMEM((2,), jnp.int32),
            vmem((TD, M), BF16), vmem((TD, W), BF16), vmem((HALO + TILES, ZH, 64, LANES), BF16),
            vmem((ZH, HALO, 64, LANES), BF16), vmem((2, 8, TD), F32), vmem((2, 256, 256), BF16),
            vmem((256, TD - LMAX), BF16), vmem((ZH, 2, NX, ZL, 8, W), F32),
            vmem((ZH, NX, ZL, 8, W), F32), vmem((ZH, NX, ZL, 8, W), F32),
            vmem((ZH, 3, ZL, 8, 256), F32), vmem((ZH, 2, NX, 8, 256), F32), vmem((ZH, 2, 2, 8, 256), F32),
            vmem((ZH, ZL, 8, 256), F32), vmem((ZH, NX, 8, 256), F32),
            vmem((ZH, 2, 8, 256), F32), vmem((ZH, 2, 8, 128), F32), vmem((ZH, 3, 8, 256), F32),
            vmem((ZH, 2, NC, 2, W), F32), vmem((ZH, NY, 2, W), F32),
            dma((6,)), dma((ZH,)), dma((ZH,)), dma((ZH,)), dma((ZH,)), dma((ZH, 3)), dma((ZH, 3)),
            dma((ZH, 4)), dma((ZH, 4)), dma((ZH, 4)), dma((ZH, 4)), dma((ZH, 3)), dma((ZH, 3)), dma((16,)), dma,
            pltpu.SemaphoreType.REGULAR((4,)),
        ],
        compiler_params=pltpu.CompilerParams(collective_id=0, has_side_effects=True,
                                             vmem_limit_bytes=40 << 20),
        name="correlate",
    )(*operands)
    return sums * scaling


def solution(mesh):
    return jax.shard_map(
        per_device,
        mesh=mesh,
        in_specs=(P("seg", None), P("seg", "lag"), P(), P()),
        out_specs=P("seg", "lag", None),
        check_vma=False,
    )
```

```python
import math

import jax
import jax.numpy as jnp
from jax import lax
from jax.experimental import pallas as pl
from jax.experimental.pallas import tpu as pltpu
from jax.sharding import PartitionSpec as P

LMAX = 1024
NX, NZ, NY, NC = 4, 16, 4, 2
ZL, ZH = 4, 4
TD, M, W = 3072, 256, 512
LANES = 128
HALO = LMAX // LANES
TILES = TD // LANES
ORDER = (0, 1, 3, 2)
F32, BF16 = jnp.float32, jnp.bfloat16


def device_at(x, z, c, y):
    return (lax.rem(x, NX) * (NZ * NC) + lax.rem(z, NZ) * NC + c, lax.rem(y, NY))


def kernel(actuators, sensors, run_lengths, lag_offsets, out,
           lengths, lags, act, sen, turned, halo, mask, shifts, lhs, part, pair, acc,
           a1, b1, b1h, sa, sb, a2, a2h, b2, stage, fin,
           in_sem, halo_s, halo_r, pair_s, pair_r, a1_s, a1_r, b1_s, b1_r,
           a2_s, a2_r, b2_s, b2_r, fin_s, fin_r, told):
    seg, y = lax.axis_index("seg"), lax.axis_index("lag")
    x, z, c = seg // (NZ * NC), lax.rem(seg // NC, NZ), lax.rem(seg, NC)
    zl, zh = lax.rem(z, ZL), z // ZL
    after = (lax.rem(seg + 1, NX * NZ * NC), y)
    before = (lax.rem(seg + NX * NZ * NC - 1, NX * NZ * NC), y)
    near = [(-1, 0), (1, 1), (2, 2), (-2, 3)]
    sibling = device_at(x, z, 1 - c, y)

    def remote(src, dst, send, recv, device):
        return pltpu.make_async_remote_copy(
            src_ref=src, dst_ref=dst, send_sem=send, recv_sem=recv,
            device_id=device, device_id_type=pl.DeviceIdType.MESH)

    barrier = pltpu.get_barrier_semaphore()

    def signal(semaphore, device):
        pl.semaphore_signal(semaphore, inc=1, device_id=device, device_id_type=pl.DeviceIdType.MESH)

    signal(barrier, before)
    loads = []
    for n, (src, dst) in enumerate([
            (actuators.at[TD - LMAX:], act.at[TD - LMAX:]), (actuators.at[:TD - LMAX], act.at[:TD - LMAX]),
            (run_lengths, lengths), (lag_offsets, lags),
            (sensors.at[LMAX:], sen.at[LMAX:]), (sensors.at[:LMAX], sen.at[:LMAX])]):
        copy = pltpu.make_async_copy(src, dst, in_sem.at[n])
        copy.start()
        loads.append(copy)
    one_hop = [device_at(x + 1, z, c, y), device_at(x + NX - 1, z, c, y), device_at(x, z + 1, c, y),
               device_at(x, z + NZ - 1, c, y), device_at(x, z, c, y + 1), device_at(x, z, c, y + NY - 1)]
    for device in [sibling] + one_hop:
        signal(barrier, device)

    rounds = [
        one_hop,
        [device_at(x, z + 2, c, y), device_at(x, z + NZ - 2, c, y), sibling],
        [device_at(x, z + 4, c, y), device_at(x, z + NZ - 4, c, y)],
        [sibling] + [device_at(x, z, cc, y + yy) for yy in range(1, NY) for cc in (c, 1 - c)],
    ]

    def tell(n):
        for device in rounds[n]:
            signal(told.at[n], device)

    def hear(n):
        pl.semaphore_wait(told.at[n], len(rounds[n]))

    row = lax.broadcasted_iota(jnp.int32, (M, M), 0)
    col = lax.broadcasted_iota(jnp.int32, (M, M), 1)
    wanted = ((row >> 4) & 3) * 64 + (row >> 6) * 16 + ((row >> 2) & 3) * 4 + (row & 3)
    order = (col == wanted).astype(F32).astype(BF16)

    def turn(k):
        flat = lax.dot_general(order, act[512 * k:512 * k + 512], (((1,), (1,)), ((), ())),
                               preferred_element_type=F32)
        for i in range(4):
            turned[HALO + 4 * k + i] = flat[:, LANES * i:LANES * i + LANES].reshape(ZH, 64, LANES).astype(BF16)

    loads[0].wait()
    turn(4)
    turn(5)
    pl.semaphore_wait(barrier, 8)
    halos = {}
    for q in ORDER:
        halos[q] = remote(turned.at[TILES:, q], halo.at[q], halo_s.at[q], halo_r.at[q], after)
        halos[q].start()
    tell(0)

    lane = lax.broadcasted_iota(jnp.int32, (8, TD), 1)
    lag_of_row = lax.broadcasted_iota(jnp.int32, (8, TD), 0) >> 2
    place = seg * TD + lane
    loads[2].wait()
    loads[3].wait()

    def step_run(b, carry):
        end, begin = carry
        end = end + lengths[b]
        return end, jnp.where(place >= end, end, begin)

    _, begin = lax.fori_loop(0, 64, step_run, (jnp.int32(0), jnp.zeros((8, TD), jnp.int32)), unroll=8)
    since = place - begin
    for b in range(2):
        mask[b] = jnp.where(since >= lags[b] + lag_of_row, 1.0, 0.0)
    for b in range(2):
        rest = (LMAX - 1 - lags[b]) & (LANES - 1)
        shifts[b] = (row == (col & (LANES - 1)) + rest + jnp.where(col < LANES, 1, 0)).astype(F32).astype(BF16)
    loads[1].wait()
    for k in range(4):
        turn(k)

    first_rows = lax.broadcasted_iota(jnp.int32, (8, 8, LANES), 1) < 4

    def build(q, first, col_at):
        for b in range(2):
            tile = ((LMAX - 1 - lags[b]) >> 7) + first
            tiles = [turned[tile + j, q] for j in range(HALO + 1)]
            windows = [jnp.concatenate(tiles[j:j + 2], axis=1) for j in range(HALO)]
            moved = jnp.dot(jnp.concatenate(windows, axis=0), shifts[b], preferred_element_type=F32)
            for j in range(HALO):
                keep = mask[b, :, LANES * (first + j):LANES * (first + j + 1)][None]
                one, two = [moved[64 * j:64 * j + 64, LANES * k:LANES * k + LANES].reshape(8, 8, LANES)
                            for k in range(2)]
                even = jnp.where(first_rows, one, pltpu.roll(two, 4, 1)) * keep
                odd = jnp.where(first_rows, pltpu.roll(one, 4, 1), two) * keep
                value = jnp.concatenate([even[:, None], odd[:, None]], axis=1).reshape(128, LANES)
                lhs[128 * b:128 * b + 128, col_at + LANES * j:col_at + LANES * (j + 1)] = value.astype(BF16)

    def own(q):
        for first in (HALO, 2 * HALO):
            build(q, first, LANES * (first - HALO))

        @pl.loop(0, 2)
        def _(n):
            cols = pl.ds(pl.multiple_of(n * 256, 256), 256)
            part[q, :, :, :, :, cols] = jnp.dot(
                lhs[...], sen[LMAX:, cols], preferred_element_type=F32).reshape(2, NX, ZL, 8, 256)

    pairs, x_first, z_first, x_second, z_second, last = {}, {}, {}, {}, {}, []

    def cross(q):
        halos[q].wait_recv()
        turned[:HALO, q] = halo[q]
        build(q, 0, 0)

        @pl.loop(0, 2)
        def _(n):
            cols = pl.ds(pl.multiple_of(n * 256, 256), 256)
            part[q, :, :, :, :, cols] += jnp.dot(
                lhs[:, :LMAX], sen[:LMAX, cols], preferred_element_type=F32).reshape(2, NX, ZL, 8, 256)

        pairs[q] = remote(part.at[q, 1 - c], pair.at[q], pair_s.at[q], pair_r.at[q], sibling)
        pairs[q].start()

    def started(copies):
        for copy in copies:
            copy.start()
        return copies

    def send_first(q):
        pairs[q].wait_recv()
        acc[q, :, :, :, :256] = part[q, c, :, :, :, :256] + pair[q, :, :, :, :256]
        x_first[q] = started([
            remote(acc.at[q, lax.rem(x + dx, NX), :, :, :256], a1.at[q, dx - 1], a1_s.at[q, dx - 1],
                   a1_r.at[q, dx - 1], device_at(x + dx, z, c, y)) for dx in (2, 1, 3)])
        acc[q, :, :, :, 256:] = part[q, c, :, :, :, 256:] + pair[q, :, :, :, 256:]
        copies = []
        for step, slot in reversed(near):
            kind = lax.rem(z + step + NZ, ZL)
            if slot < 2:
                src, dst = acc.at[q, :, kind, :, 256:], b1.at[q, slot]
            else:
                src, dst = acc.at[q, 2 * (slot - 2):2 * (slot - 1), kind, :, 256:], b1h.at[q, slot - 2]
            copies.append(remote(src, dst, b1_s.at[q, slot], b1_r.at[q, slot],
                                 device_at(x, z + step + NZ, c, y)))
        z_first[q] = started(copies)

    def send_second(q):
        for copy in x_first[q]:
            copy.wait_recv()
        for zz in range(ZL):
            sa[q, zz] = (acc[q, x, zz, :, :256] + a1[q, 0, zz]) + (a1[q, 1, zz] + a1[q, 2, zz])
        copies = []
        for step, slot in reversed(near):
            kind = lax.rem(z + step + NZ, ZL)
            if slot < 2:
                src, dst = sa.at[q, kind], a2.at[q, slot]
            else:
                src, dst = sa.at[q, kind, :, 128 * (slot - 2):128 * (slot - 1)], a2h.at[q, slot - 2]
            copies.append(remote(src, dst, a2_s.at[q, slot], a2_r.at[q, slot],
                                 device_at(x, z + step + NZ, c, y)))
        z_second[q] = started(copies)
        for copy in z_first[q]:
            copy.wait_recv()
        for xx in range(NX):
            sb[q, xx] = ((acc[q, xx, zl, :, 256:] + b1[q, 0, xx]) + (b1[q, 1, xx] + b1h[q, xx // 2, xx % 2]))
        x_second[q] = started([
            remote(sb.at[q, lax.rem(x + dx, NX)], b2.at[q, dx - 1], b2_s.at[q, dx - 1], b2_r.at[q, dx - 1],
                   device_at(x + dx, z, c, y)) for dx in (2, 1, 3)])

    def send_third(q):
        for copy in z_second[q]:
            copy.wait_recv()
        left = (sa[q, zl] + a2[q, 0]) + (a2[q, 1] + jnp.concatenate([a2h[q, 0], a2h[q, 1]], axis=1))
        for copy in x_second[q]:
            copy.wait_recv()
        right = (sb[q, x] + b2[q, 0]) + (b2[q, 1] + b2[q, 2])
        total = jnp.concatenate([left, right], axis=1)
        for k in range(2):
            for cc in range(NC):
                stage[q, k, cc] = total[4 * k + 2 * cc:4 * k + 2 * cc + 2]
                src, dst = stage.at[q, k, cc], fin.at[zh, y]
                copy = remote(src, dst, fin_s.at[4 * q + 2 * k + cc], fin_r,
                              device_at(x, ZL * q + zl, cc, 2 * c + k))
                mine = (cc == c) & (y == 2 * c + k) & (zh == q)

                @pl.when(mine)
                def _():
                    pltpu.make_async_copy(src, dst, fin_r).start()

                @pl.when(jnp.logical_not(mine))
                def _():
                    copy.start()
                last.append((copy, mine))

    q0, q1, q2, q3 = ORDER
    loads[4].wait()
    own(q0)
    hear(0)
    tell(1)
    loads[5].wait()
    cross(q0)
    own(q1)
    send_first(q0)
    hear(1)
    tell(2)
    cross(q1)
    own(q2)
    send_first(q1)
    cross(q2)
    send_second(q0)
    hear(2)
    tell(3)
    own(q3)
    send_first(q2)
    hear(3)
    send_third(q0)
    send_second(q1)
    cross(q3)
    send_first(q3)
    send_third(q1)
    send_second(q2)
    send_third(q2)
    send_second(q3)
    send_third(q3)
    for q in ORDER:
        for copy in [halos[q], pairs[q]] + x_first[q] + z_first[q] + x_second[q] + z_second[q]:
            copy.wait_send()
    pltpu.make_async_copy(fin, fin, fin_r).wait()
    for yy in range(NY):
        total = (fin[0, yy] + fin[1, yy]) + (fin[2, yy] + fin[3, yy])
        for j in range(2):
            out[j, :, W * yy:W * (yy + 1)] = total[j:j + 1]
    for copy, mine in last:
        pl.when(jnp.logical_not(mine))(copy.wait_send)


def per_device(actuator_input, sensor_output, run_lengths, lag_offsets):
    samples = actuator_input.shape[0]
    scaling = 1.0 / math.sqrt(samples * lax.axis_size("seg"))
    dma, vmem = pltpu.SemaphoreType.DMA, pltpu.VMEM
    operands = [pltpu.with_memory_space_constraint(operand, pltpu.HBM)
                for operand in (actuator_input, sensor_output, run_lengths, lag_offsets)]
    sums = pl.pallas_call(
        kernel,
        out_shape=jax.ShapeDtypeStruct((2, 1, NY * W), F32),
        in_specs=[pl.BlockSpec(memory_space=pltpu.HBM)] * 4,
        out_specs=pl.BlockSpec(memory_space=pltpu.VMEM),
        scratch_shapes=[
            pltpu.SMEM((64,), jnp.int32), pltpu.SMEM((2,), jnp.int32),
            vmem((TD, M), BF16), vmem((TD, W), BF16), vmem((HALO + TILES, ZH, 64, LANES), BF16),
            vmem((ZH, HALO, 64, LANES), BF16), vmem((2, 8, TD), F32), vmem((2, 256, 256), BF16),
            vmem((256, TD - LMAX), BF16), vmem((ZH, 2, NX, ZL, 8, W), F32),
            vmem((ZH, NX, ZL, 8, W), F32), vmem((ZH, NX, ZL, 8, W), F32),
            vmem((ZH, 3, ZL, 8, 256), F32), vmem((ZH, 2, NX, 8, 256), F32), vmem((ZH, 2, 2, 8, 256), F32),
            vmem((ZH, ZL, 8, 256), F32), vmem((ZH, NX, 8, 256), F32),
            vmem((ZH, 2, 8, 256), F32), vmem((ZH, 2, 8, 128), F32), vmem((ZH, 3, 8, 256), F32),
            vmem((ZH, 2, NC, 2, W), F32), vmem((ZH, NY, 2, W), F32),
            dma((6,)), dma((ZH,)), dma((ZH,)), dma((ZH,)), dma((ZH,)), dma((ZH, 3)), dma((ZH, 3)),
            dma((ZH, 4)), dma((ZH, 4)), dma((ZH, 4)), dma((ZH, 4)), dma((ZH, 3)), dma((ZH, 3)), dma((16,)), dma,
            pltpu.SemaphoreType.REGULAR((4,)),
        ],
        compiler_params=pltpu.CompilerParams(collective_id=0, has_side_effects=True,
                                             vmem_limit_bytes=40 << 20),
        name="correlate",
    )(*operands)
    return sums * scaling


def solution(mesh):
    return jax.shard_map(
        per_device,
        mesh=mesh,
        in_specs=(P("seg", None), P("seg", "lag"), P(), P()),
        out_specs=P("seg", "lag", None),
        check_vma=False,
    )
```

```python
import math

import jax
import jax.numpy as jnp
from jax import lax
from jax.experimental import pallas as pl
from jax.experimental.pallas import tpu as pltpu
from jax.sharding import PartitionSpec as P

LMAX = 1024
NX, NZ, NY, NC = 4, 16, 4, 2
ZL, ZH = 4, 4
TD, M, W = 3072, 256, 512
LANES = 128
HALO = LMAX // LANES
TILES = TD // LANES
ORDER = (0, 1, 3, 2)
F32, BF16 = jnp.float32, jnp.bfloat16


def device_at(x, z, c, y):
    return (lax.rem(x, NX) * (NZ * NC) + lax.rem(z, NZ) * NC + c, lax.rem(y, NY))


def kernel(actuators, sensors, run_lengths, lag_offsets, out,
           lengths, lags, act, sen, turned, halo, mask, shifts, lhs, part, pair, acc,
           a1, b1, b1h, sa, sb, a2, a2h, b2, stage, fin,
           in_sem, halo_s, halo_r, pair_s, pair_r, a1_s, a1_r, b1_s, b1_r,
           a2_s, a2_r, b2_s, b2_r, fin_s, fin_r, told):
    seg, y = lax.axis_index("seg"), lax.axis_index("lag")
    x, z, c = seg // (NZ * NC), lax.rem(seg // NC, NZ), lax.rem(seg, NC)
    zl, zh = lax.rem(z, ZL), z // ZL
    after = (lax.rem(seg + 1, NX * NZ * NC), y)
    before = (lax.rem(seg + NX * NZ * NC - 1, NX * NZ * NC), y)
    near = [(-1, 0), (1, 1), (2, 2), (-2, 3)]
    sibling = device_at(x, z, 1 - c, y)

    def remote(src, dst, send, recv, device):
        return pltpu.make_async_remote_copy(
            src_ref=src, dst_ref=dst, send_sem=send, recv_sem=recv,
            device_id=device, device_id_type=pl.DeviceIdType.MESH)

    barrier = pltpu.get_barrier_semaphore()

    def signal(semaphore, device):
        pl.semaphore_signal(semaphore, inc=1, device_id=device, device_id_type=pl.DeviceIdType.MESH)

    signal(barrier, before)
    loads = []
    for n, (src, dst) in enumerate([
            (actuators.at[TD - LMAX:], act.at[TD - LMAX:]), (actuators.at[:TD - LMAX], act.at[:TD - LMAX]),
            (run_lengths, lengths), (lag_offsets, lags),
            (sensors.at[LMAX:], sen.at[LMAX:]), (sensors.at[:LMAX], sen.at[:LMAX])]):
        copy = pltpu.make_async_copy(src, dst, in_sem.at[n])
        copy.start()
        loads.append(copy)
    one_hop = [device_at(x + 1, z, c, y), device_at(x + NX - 1, z, c, y), device_at(x, z + 1, c, y),
               device_at(x, z + NZ - 1, c, y), device_at(x, z, c, y + 1), device_at(x, z, c, y + NY - 1)]
    for device in [sibling] + one_hop:
        signal(barrier, device)

    rounds = [
        one_hop,
        [device_at(x, z + 2, c, y), device_at(x, z + NZ - 2, c, y), sibling],
        [device_at(x, z + 4, c, y), device_at(x, z + NZ - 4, c, y)],
        [sibling] + [device_at(x, z, cc, y + yy) for yy in range(1, NY) for cc in (c, 1 - c)],
    ]

    def tell(n):
        for device in rounds[n]:
            signal(told.at[n], device)

    def hear(n):
        pl.semaphore_wait(told.at[n], len(rounds[n]))

    row = lax.broadcasted_iota(jnp.int32, (M, M), 0)
    col = lax.broadcasted_iota(jnp.int32, (M, M), 1)
    wanted = ((row >> 4) & 3) * 64 + (row >> 6) * 16 + ((row >> 2) & 3) * 4 + (row & 3)
    order = (col == wanted).astype(F32).astype(BF16)

    def turn(k):
        flat = lax.dot_general(order, act[512 * k:512 * k + 512], (((1,), (1,)), ((), ())),
                               preferred_element_type=F32)
        for i in range(4):
            turned[HALO + 4 * k + i] = flat[:, LANES * i:LANES * i + LANES].reshape(ZH, 64, LANES).astype(BF16)

    loads[0].wait()
    turn(4)
    turn(5)
    pl.semaphore_wait(barrier, 8)
    halos = {}
    for q in ORDER:
        halos[q] = remote(turned.at[TILES:, q], halo.at[q], halo_s.at[q], halo_r.at[q], after)
        halos[q].start()
    tell(0)

    lane = lax.broadcasted_iota(jnp.int32, (8, TD), 1)
    lag_of_row = lax.broadcasted_iota(jnp.int32, (8, TD), 0) >> 2
    place = seg * TD + lane
    loads[2].wait()
    loads[3].wait()

    def step_run(b, carry):
        end, begin = carry
        end = end + lengths[b]
        return end, jnp.where(place >= end, end, begin)

    _, begin = lax.fori_loop(0, 64, step_run, (jnp.int32(0), jnp.zeros((8, TD), jnp.int32)), unroll=8)
    since = place - begin
    for b in range(2):
        mask[b] = jnp.where(since >= lags[b] + lag_of_row, 1.0, 0.0)
    for b in range(2):
        rest = (LMAX - 1 - lags[b]) & (LANES - 1)
        shifts[b] = (row == (col & (LANES - 1)) + rest + jnp.where(col < LANES, 1, 0)).astype(F32).astype(BF16)
    loads[1].wait()
    for k in range(4):
        turn(k)

    first_rows = lax.broadcasted_iota(jnp.int32, (8, 8, LANES), 1) < 4

    def build(q, first, col_at):
        for b in range(2):
            tile = ((LMAX - 1 - lags[b]) >> 7) + first
            tiles = [turned[tile + j, q] for j in range(HALO + 1)]
            windows = [jnp.concatenate(tiles[j:j + 2], axis=1) for j in range(HALO)]
            moved = jnp.dot(jnp.concatenate(windows, axis=0), shifts[b], preferred_element_type=F32)
            for j in range(HALO):
                keep = mask[b, :, LANES * (first + j):LANES * (first + j + 1)][None]
                one, two = [moved[64 * j:64 * j + 64, LANES * k:LANES * k + LANES].reshape(8, 8, LANES)
                            for k in range(2)]
                even = jnp.where(first_rows, one, pltpu.roll(two, 4, 1)) * keep
                odd = jnp.where(first_rows, pltpu.roll(one, 4, 1), two) * keep
                value = jnp.concatenate([even[:, None], odd[:, None]], axis=1).reshape(128, LANES)
                lhs[128 * b:128 * b + 128, col_at + LANES * j:col_at + LANES * (j + 1)] = value.astype(BF16)

    def own(q):
        for first in (HALO, 2 * HALO):
            build(q, first, LANES * (first - HALO))

        @pl.loop(0, 2)
        def _(n):
            cols = pl.ds(pl.multiple_of(n * 256, 256), 256)
            part[q, :, :, :, :, cols] = jnp.dot(
                lhs[...], sen[LMAX:, cols], preferred_element_type=F32).reshape(2, NX, ZL, 8, 256)

    pairs, x_first, z_first, x_second, z_second, last = {}, {}, {}, {}, {}, []

    def cross(q):
        halos[q].wait_recv()
        turned[:HALO, q] = halo[q]
        build(q, 0, 0)

        @pl.loop(0, 2)
        def _(n):
            cols = pl.ds(pl.multiple_of(n * 256, 256), 256)
            part[q, :, :, :, :, cols] += jnp.dot(
                lhs[:, :LMAX], sen[:LMAX, cols], preferred_element_type=F32).reshape(2, NX, ZL, 8, 256)

        pairs[q] = remote(part.at[q, 1 - c], pair.at[q], pair_s.at[q], pair_r.at[q], sibling)
        pairs[q].start()

    def started(copies):
        for copy in copies:
            copy.start()
        return copies

    def send_first(q):
        pairs[q].wait_recv()
        acc[q, :, :, :, :256] = part[q, c, :, :, :, :256] + pair[q, :, :, :, :256]
        x_first[q] = started([
            remote(acc.at[q, lax.rem(x + dx, NX), :, :, :256], a1.at[q, dx - 1], a1_s.at[q, dx - 1],
                   a1_r.at[q, dx - 1], device_at(x + dx, z, c, y)) for dx in (2, 1, 3)])
        acc[q, :, :, :, 256:] = part[q, c, :, :, :, 256:] + pair[q, :, :, :, 256:]
        copies = []
        for step, slot in reversed(near):
            kind = lax.rem(z + step + NZ, ZL)
            if slot < 2:
                src, dst = acc.at[q, :, kind, :, 256:], b1.at[q, slot]
            else:
                src, dst = acc.at[q, 2 * (slot - 2):2 * (slot - 1), kind, :, 256:], b1h.at[q, slot - 2]
            copies.append(remote(src, dst, b1_s.at[q, slot], b1_r.at[q, slot],
                                 device_at(x, z + step + NZ, c, y)))
        z_first[q] = started(copies)

    def send_second(q):
        for copy in x_first[q]:
            copy.wait_recv()
        for zz in range(ZL):
            sa[q, zz] = (acc[q, x, zz, :, :256] + a1[q, 0, zz]) + (a1[q, 1, zz] + a1[q, 2, zz])
        copies = []
        for step, slot in reversed(near):
            kind = lax.rem(z + step + NZ, ZL)
            if slot < 2:
                src, dst = sa.at[q, kind], a2.at[q, slot]
            else:
                src, dst = sa.at[q, kind, :, 128 * (slot - 2):128 * (slot - 1)], a2h.at[q, slot - 2]
            copies.append(remote(src, dst, a2_s.at[q, slot], a2_r.at[q, slot],
                                 device_at(x, z + step + NZ, c, y)))
        z_second[q] = started(copies)
        for copy in z_first[q]:
            copy.wait_recv()
        for xx in range(NX):
            sb[q, xx] = ((acc[q, xx, zl, :, 256:] + b1[q, 0, xx]) + (b1[q, 1, xx] + b1h[q, xx // 2, xx % 2]))
        x_second[q] = started([
            remote(sb.at[q, lax.rem(x + dx, NX)], b2.at[q, dx - 1], b2_s.at[q, dx - 1], b2_r.at[q, dx - 1],
                   device_at(x + dx, z, c, y)) for dx in (2, 1, 3)])

    def send_third(q):
        for copy in z_second[q]:
            copy.wait_recv()
        left = (sa[q, zl] + a2[q, 0]) + (a2[q, 1] + jnp.concatenate([a2h[q, 0], a2h[q, 1]], axis=1))
        for copy in x_second[q]:
            copy.wait_recv()
        right = (sb[q, x] + b2[q, 0]) + (b2[q, 1] + b2[q, 2])
        total = jnp.concatenate([left, right], axis=1)
        for k in range(2):
            for cc in range(NC):
                stage[q, k, cc] = total[4 * k + 2 * cc:4 * k + 2 * cc + 2]
                src, dst = stage.at[q, k, cc], fin.at[zh, y]
                copy = remote(src, dst, fin_s.at[4 * q + 2 * k + cc], fin_r,
                              device_at(x, ZL * q + zl, cc, 2 * c + k))
                mine = (cc == c) & (y == 2 * c + k) & (zh == q)

                @pl.when(mine)
                def _():
                    pltpu.make_async_copy(src, dst, fin_r).start()

                @pl.when(jnp.logical_not(mine))
                def _():
                    copy.start()
                last.append((copy, mine))

    q0, q1, q2, q3 = ORDER
    loads[4].wait()
    own(q0)
    hear(0)
    tell(1)
    loads[5].wait()
    cross(q0)
    own(q1)
    send_first(q0)
    hear(1)
    tell(2)
    cross(q1)
    own(q2)
    send_first(q1)
    cross(q2)
    own(q3)
    send_second(q0)
    hear(2)
    tell(3)
    send_first(q2)
    cross(q3)
    send_second(q1)
    send_first(q3)
    hear(3)
    send_third(q0)
    send_second(q2)
    send_third(q1)
    send_second(q3)
    send_third(q2)
    send_third(q3)
    for q in ORDER:
        for copy in [halos[q], pairs[q]] + x_first[q] + z_first[q] + x_second[q] + z_second[q]:
            copy.wait_send()
    pltpu.make_async_copy(fin, fin, fin_r).wait()
    for yy in range(NY):
        total = (fin[0, yy] + fin[1, yy]) + (fin[2, yy] + fin[3, yy])
        for j in range(2):
            out[j, :, W * yy:W * (yy + 1)] = total[j:j + 1]
    for copy, mine in last:
        pl.when(jnp.logical_not(mine))(copy.wait_send)


def per_device(actuator_input, sensor_output, run_lengths, lag_offsets):
    samples = actuator_input.shape[0]
    scaling = 1.0 / math.sqrt(samples * lax.axis_size("seg"))
    dma, vmem = pltpu.SemaphoreType.DMA, pltpu.VMEM
    operands = [pltpu.with_memory_space_constraint(operand, pltpu.HBM)
                for operand in (actuator_input, sensor_output, run_lengths, lag_offsets)]
    sums = pl.pallas_call(
        kernel,
        out_shape=jax.ShapeDtypeStruct((2, 1, NY * W), F32),
        in_specs=[pl.BlockSpec(memory_space=pltpu.HBM)] * 4,
        out_specs=pl.BlockSpec(memory_space=pltpu.VMEM),
        scratch_shapes=[
            pltpu.SMEM((64,), jnp.int32), pltpu.SMEM((2,), jnp.int32),
            vmem((TD, M), BF16), vmem((TD, W), BF16), vmem((HALO + TILES, ZH, 64, LANES), BF16),
            vmem((ZH, HALO, 64, LANES), BF16), vmem((2, 8, TD), F32), vmem((2, 256, 256), BF16),
            vmem((256, TD - LMAX), BF16), vmem((ZH, 2, NX, ZL, 8, W), F32),
            vmem((ZH, NX, ZL, 8, W), F32), vmem((ZH, NX, ZL, 8, W), F32),
            vmem((ZH, 3, ZL, 8, 256), F32), vmem((ZH, 2, NX, 8, 256), F32), vmem((ZH, 2, 2, 8, 256), F32),
            vmem((ZH, ZL, 8, 256), F32), vmem((ZH, NX, 8, 256), F32),
            vmem((ZH, 2, 8, 256), F32), vmem((ZH, 2, 8, 128), F32), vmem((ZH, 3, 8, 256), F32),
            vmem((ZH, 2, NC, 2, W), F32), vmem((ZH, NY, 2, W), F32),
            dma((6,)), dma((ZH,)), dma((ZH,)), dma((ZH,)), dma((ZH,)), dma((ZH, 3)), dma((ZH, 3)),
            dma((ZH, 4)), dma((ZH, 4)), dma((ZH, 4)), dma((ZH, 4)), dma((ZH, 3)), dma((ZH, 3)), dma((16,)), dma,
            pltpu.SemaphoreType.REGULAR((4,)),
        ],
        compiler_params=pltpu.CompilerParams(collective_id=0, has_side_effects=True,
                                             vmem_limit_bytes=40 << 20),
        name="correlate",
    )(*operands)
    return sums * scaling


def solution(mesh):
    return jax.shard_map(
        per_device,
        mesh=mesh,
        in_specs=(P("seg", None), P("seg", "lag"), P(), P()),
        out_specs=P("seg", "lag", None),
        check_vma=False,
    )
```

```python
import math

import jax
import jax.numpy as jnp
from jax import lax
from jax.experimental import pallas as pl
from jax.experimental.pallas import tpu as pltpu
from jax.sharding import PartitionSpec as P

LMAX = 1024
NX, NZ, NY, NC = 4, 16, 4, 2
ZL, ZH = 4, 4
TD, M, W = 3072, 256, 512
LANES = 128
HALO = LMAX // LANES
TILES = TD // LANES
ORDER = (0, 1, 3, 2)
F32, BF16 = jnp.float32, jnp.bfloat16


def device_at(x, z, c, y):
    return (lax.rem(x, NX) * (NZ * NC) + lax.rem(z, NZ) * NC + c, lax.rem(y, NY))


def kernel(actuators, sensors, run_lengths, lag_offsets, out,
           lengths, lags, act, sen, turned, halo, mask, shifts, lhs, part, pair, acc,
           a1, b1, b1h, sa, sb, a2, a2h, b2, stage, fin,
           in_sem, halo_s, halo_r, pair_s, pair_r, a1_s, a1_r, b1_s, b1_r,
           a2_s, a2_r, b2_s, b2_r, fin_s, fin_r, told):
    seg, y = lax.axis_index("seg"), lax.axis_index("lag")
    x, z, c = seg // (NZ * NC), lax.rem(seg // NC, NZ), lax.rem(seg, NC)
    zl, zh = lax.rem(z, ZL), z // ZL
    after = (lax.rem(seg + 1, NX * NZ * NC), y)
    before = (lax.rem(seg + NX * NZ * NC - 1, NX * NZ * NC), y)
    near = [(-1, 0), (1, 1), (2, 2), (-2, 3)]
    sibling = device_at(x, z, 1 - c, y)

    def remote(src, dst, send, recv, device):
        return pltpu.make_async_remote_copy(
            src_ref=src, dst_ref=dst, send_sem=send, recv_sem=recv,
            device_id=device, device_id_type=pl.DeviceIdType.MESH)

    barrier = pltpu.get_barrier_semaphore()

    def signal(semaphore, device):
        pl.semaphore_signal(semaphore, inc=1, device_id=device, device_id_type=pl.DeviceIdType.MESH)

    signal(barrier, before)
    loads = []
    for n, (src, dst) in enumerate([
            (actuators.at[TD - LMAX:], act.at[TD - LMAX:]), (actuators.at[:TD - LMAX], act.at[:TD - LMAX]),
            (run_lengths, lengths), (lag_offsets, lags),
            (sensors.at[LMAX:], sen.at[LMAX:]), (sensors.at[:LMAX], sen.at[:LMAX])]):
        copy = pltpu.make_async_copy(src, dst, in_sem.at[n])
        copy.start()
        loads.append(copy)
    one_hop = [device_at(x + 1, z, c, y), device_at(x + NX - 1, z, c, y), device_at(x, z + 1, c, y),
               device_at(x, z + NZ - 1, c, y), device_at(x, z, c, y + 1), device_at(x, z, c, y + NY - 1)]
    for device in [sibling] + one_hop:
        signal(barrier, device)

    rounds = [
        one_hop,
        [device_at(x, z + 2, c, y), device_at(x, z + NZ - 2, c, y), sibling],
        [device_at(x, z + 4, c, y), device_at(x, z + NZ - 4, c, y)],
        [sibling] + [device_at(x, z, cc, y + yy) for yy in range(1, NY) for cc in (c, 1 - c)],
    ]

    def tell(n):
        for device in rounds[n]:
            signal(told.at[n], device)

    def hear(n):
        pl.semaphore_wait(told.at[n], len(rounds[n]))

    row = lax.broadcasted_iota(jnp.int32, (M, M), 0)
    col = lax.broadcasted_iota(jnp.int32, (M, M), 1)
    wanted = ((row >> 4) & 3) * 64 + (row >> 6) * 16 + ((row >> 2) & 3) * 4 + (row & 3)
    order = (col == wanted).astype(F32).astype(BF16)

    def turn(k):
        flat = lax.dot_general(order, act[512 * k:512 * k + 512], (((1,), (1,)), ((), ())),
                               preferred_element_type=F32)
        for i in range(4):
            turned[HALO + 4 * k + i] = flat[:, LANES * i:LANES * i + LANES].reshape(ZH, 64, LANES).astype(BF16)

    loads[0].wait()
    turn(4)
    turn(5)
    lane = lax.broadcasted_iota(jnp.int32, (8, TD), 1)
    lag_of_row = lax.broadcasted_iota(jnp.int32, (8, TD), 0) >> 2
    place = seg * TD + lane
    loads[2].wait()
    loads[3].wait()

    def step_run(b, carry):
        end, begin = carry
        end = end + lengths[b]
        return end, jnp.where(place >= end, end, begin)

    _, begin = lax.fori_loop(0, 64, step_run, (jnp.int32(0), jnp.zeros((8, TD), jnp.int32)), unroll=8)
    since = place - begin
    for b in range(2):
        mask[b] = jnp.where(since >= lags[b] + lag_of_row, 1.0, 0.0)
    for b in range(2):
        rest = (LMAX - 1 - lags[b]) & (LANES - 1)
        shifts[b] = (row == (col & (LANES - 1)) + rest + jnp.where(col < LANES, 1, 0)).astype(F32).astype(BF16)
    pl.semaphore_wait(barrier, 8)
    halos = {}
    for q in ORDER:
        halos[q] = remote(turned.at[TILES:, q], halo.at[q], halo_s.at[q], halo_r.at[q], after)
        halos[q].start()
    tell(0)

    loads[1].wait()
    for k in range(4):
        turn(k)

    first_rows = lax.broadcasted_iota(jnp.int32, (8, 8, LANES), 1) < 4

    def build(q, first, col_at):
        for b in range(2):
            tile = ((LMAX - 1 - lags[b]) >> 7) + first
            tiles = [turned[tile + j, q] for j in range(HALO + 1)]
            windows = [jnp.concatenate(tiles[j:j + 2], axis=1) for j in range(HALO)]
            moved = jnp.dot(jnp.concatenate(windows, axis=0), shifts[b], preferred_element_type=F32)
            for j in range(HALO):
                keep = mask[b, :, LANES * (first + j):LANES * (first + j + 1)][None]
                one, two = [moved[64 * j:64 * j + 64, LANES * k:LANES * k + LANES].reshape(8, 8, LANES)
                            for k in range(2)]
                even = jnp.where(first_rows, one, pltpu.roll(two, 4, 1)) * keep
                odd = jnp.where(first_rows, pltpu.roll(one, 4, 1), two) * keep
                value = jnp.concatenate([even[:, None], odd[:, None]], axis=1).reshape(128, LANES)
                lhs[128 * b:128 * b + 128, col_at + LANES * j:col_at + LANES * (j + 1)] = value.astype(BF16)

    def own(q):
        for first in (HALO, 2 * HALO):
            build(q, first, LANES * (first - HALO))

        @pl.loop(0, 2)
        def _(n):
            cols = pl.ds(pl.multiple_of(n * 256, 256), 256)
            part[q, :, :, :, :, cols] = jnp.dot(
                lhs[...], sen[LMAX:, cols], preferred_element_type=F32).reshape(2, NX, ZL, 8, 256)

    pairs, x_first, z_first, x_second, z_second, last = {}, {}, {}, {}, {}, []

    def cross(q):
        halos[q].wait_recv()
        turned[:HALO, q] = halo[q]
        build(q, 0, 0)

        @pl.loop(0, 2)
        def _(n):
            cols = pl.ds(pl.multiple_of(n * 256, 256), 256)
            part[q, :, :, :, :, cols] += jnp.dot(
                lhs[:, :LMAX], sen[:LMAX, cols], preferred_element_type=F32).reshape(2, NX, ZL, 8, 256)

        pairs[q] = remote(part.at[q, 1 - c], pair.at[q], pair_s.at[q], pair_r.at[q], sibling)
        pairs[q].start()

    def started(copies):
        for copy in copies:
            copy.start()
        return copies

    def send_first(q):
        pairs[q].wait_recv()
        acc[q, :, :, :, :256] = part[q, c, :, :, :, :256] + pair[q, :, :, :, :256]
        x_first[q] = started([
            remote(acc.at[q, lax.rem(x + dx, NX), :, :, :256], a1.at[q, dx - 1], a1_s.at[q, dx - 1],
                   a1_r.at[q, dx - 1], device_at(x + dx, z, c, y)) for dx in (2, 1, 3)])
        acc[q, :, :, :, 256:] = part[q, c, :, :, :, 256:] + pair[q, :, :, :, 256:]
        copies = []
        for step, slot in reversed(near):
            kind = lax.rem(z + step + NZ, ZL)
            if slot < 2:
                src, dst = acc.at[q, :, kind, :, 256:], b1.at[q, slot]
            else:
                src, dst = acc.at[q, 2 * (slot - 2):2 * (slot - 1), kind, :, 256:], b1h.at[q, slot - 2]
            copies.append(remote(src, dst, b1_s.at[q, slot], b1_r.at[q, slot],
                                 device_at(x, z + step + NZ, c, y)))
        z_first[q] = started(copies)

    def send_second(q):
        for copy in x_first[q]:
            copy.wait_recv()
        for zz in range(ZL):
            sa[q, zz] = (acc[q, x, zz, :, :256] + a1[q, 0, zz]) + (a1[q, 1, zz] + a1[q, 2, zz])
        copies = []
        for step, slot in reversed(near):
            kind = lax.rem(z + step + NZ, ZL)
            if slot < 2:
                src, dst = sa.at[q, kind], a2.at[q, slot]
            else:
                src, dst = sa.at[q, kind, :, 128 * (slot - 2):128 * (slot - 1)], a2h.at[q, slot - 2]
            copies.append(remote(src, dst, a2_s.at[q, slot], a2_r.at[q, slot],
                                 device_at(x, z + step + NZ, c, y)))
        z_second[q] = started(copies)
        for copy in z_first[q]:
            copy.wait_recv()
        for xx in range(NX):
            sb[q, xx] = ((acc[q, xx, zl, :, 256:] + b1[q, 0, xx]) + (b1[q, 1, xx] + b1h[q, xx // 2, xx % 2]))
        x_second[q] = started([
            remote(sb.at[q, lax.rem(x + dx, NX)], b2.at[q, dx - 1], b2_s.at[q, dx - 1], b2_r.at[q, dx - 1],
                   device_at(x + dx, z, c, y)) for dx in (2, 1, 3)])

    def send_third(q):
        for copy in z_second[q]:
            copy.wait_recv()
        left = (sa[q, zl] + a2[q, 0]) + (a2[q, 1] + jnp.concatenate([a2h[q, 0], a2h[q, 1]], axis=1))
        for copy in x_second[q]:
            copy.wait_recv()
        right = (sb[q, x] + b2[q, 0]) + (b2[q, 1] + b2[q, 2])
        total = jnp.concatenate([left, right], axis=1)
        for k in range(2):
            for cc in range(NC):
                stage[q, k, cc] = total[4 * k + 2 * cc:4 * k + 2 * cc + 2]
                src, dst = stage.at[q, k, cc], fin.at[zh, y]
                copy = remote(src, dst, fin_s.at[4 * q + 2 * k + cc], fin_r,
                              device_at(x, ZL * q + zl, cc, 2 * c + k))
                mine = (cc == c) & (y == 2 * c + k) & (zh == q)

                @pl.when(mine)
                def _():
                    pltpu.make_async_copy(src, dst, fin_r).start()

                @pl.when(jnp.logical_not(mine))
                def _():
                    copy.start()
                last.append((copy, mine))

    q0, q1, q2, q3 = ORDER
    loads[4].wait()
    own(q0)
    own(q1)
    hear(0)
    tell(1)
    loads[5].wait()
    cross(q0)
    own(q2)
    send_first(q0)
    hear(1)
    tell(2)
    cross(q1)
    own(q3)
    send_first(q1)
    cross(q2)
    cross(q3)
    send_second(q0)
    hear(2)
    tell(3)
    send_first(q2)
    send_first(q3)
    send_second(q1)
    hear(3)
    send_third(q0)
    send_second(q2)
    send_third(q1)
    send_second(q3)
    send_third(q2)
    send_third(q3)
    for q in ORDER:
        for copy in [halos[q], pairs[q]] + x_first[q] + z_first[q] + x_second[q] + z_second[q]:
            copy.wait_send()
    pltpu.make_async_copy(fin, fin, fin_r).wait()
    for yy in range(NY):
        total = (fin[0, yy] + fin[1, yy]) + (fin[2, yy] + fin[3, yy])
        for j in range(2):
            out[j, :, W * yy:W * (yy + 1)] = total[j:j + 1]
    for copy, mine in last:
        pl.when(jnp.logical_not(mine))(copy.wait_send)


def per_device(actuator_input, sensor_output, run_lengths, lag_offsets):
    samples = actuator_input.shape[0]
    scaling = 1.0 / math.sqrt(samples * lax.axis_size("seg"))
    dma, vmem = pltpu.SemaphoreType.DMA, pltpu.VMEM
    operands = [pltpu.with_memory_space_constraint(operand, pltpu.HBM)
                for operand in (actuator_input, sensor_output, run_lengths, lag_offsets)]
    sums = pl.pallas_call(
        kernel,
        out_shape=jax.ShapeDtypeStruct((2, 1, NY * W), F32),
        in_specs=[pl.BlockSpec(memory_space=pltpu.HBM)] * 4,
        out_specs=pl.BlockSpec(memory_space=pltpu.VMEM),
        scratch_shapes=[
            pltpu.SMEM((64,), jnp.int32), pltpu.SMEM((2,), jnp.int32),
            vmem((TD, M), BF16), vmem((TD, W), BF16), vmem((HALO + TILES, ZH, 64, LANES), BF16),
            vmem((ZH, HALO, 64, LANES), BF16), vmem((2, 8, TD), F32), vmem((2, 256, 256), BF16),
            vmem((256, TD - LMAX), BF16), vmem((ZH, 2, NX, ZL, 8, W), F32),
            vmem((ZH, NX, ZL, 8, W), F32), vmem((ZH, NX, ZL, 8, W), F32),
            vmem((ZH, 3, ZL, 8, 256), F32), vmem((ZH, 2, NX, 8, 256), F32), vmem((ZH, 2, 2, 8, 256), F32),
            vmem((ZH, ZL, 8, 256), F32), vmem((ZH, NX, 8, 256), F32),
            vmem((ZH, 2, 8, 256), F32), vmem((ZH, 2, 8, 128), F32), vmem((ZH, 3, 8, 256), F32),
            vmem((ZH, 2, NC, 2, W), F32), vmem((ZH, NY, 2, W), F32),
            dma((6,)), dma((ZH,)), dma((ZH,)), dma((ZH,)), dma((ZH,)), dma((ZH, 3)), dma((ZH, 3)),
            dma((ZH, 4)), dma((ZH, 4)), dma((ZH, 4)), dma((ZH, 4)), dma((ZH, 3)), dma((ZH, 3)), dma((16,)), dma,
            pltpu.SemaphoreType.REGULAR((4,)),
        ],
        compiler_params=pltpu.CompilerParams(collective_id=0, has_side_effects=True,
                                             vmem_limit_bytes=40 << 20),
        name="correlate",
    )(*operands)
    return sums * scaling


def solution(mesh):
    return jax.shard_map(
        per_device,
        mesh=mesh,
        in_specs=(P("seg", None), P("seg", "lag"), P(), P()),
        out_specs=P("seg", "lag", None),
        check_vma=False,
    )
```
